32 devices in a mesh: gx: 4 (over y, core), gy: 2 (over x), gz: 4 (over z).
Axes of the slice: x: 2, y: 2, z: 4, core: 2. Of those that a mesh axis runs over, the one named last changes fastest.
Arguments:
- offsets: float32 [8, 4, 8, 3, 128], P('gx', 'gy', 'gz'), may hold values from 0 to 1
- velocity: float32 [8, 4, 8, 3, 128], P('gx', 'gy', 'gz'), may hold values from -6 to 6
- mass: float32 [8, 4, 8, 128], P('gx', 'gy', 'gz'), may hold values from 0.05 to 0.2
- energy: float32 [8, 4, 8, 128], P('gx', 'gy', 'gz'), may hold values from 0.5 to 2
- partner_mask: int32 [8, 4, 8, 27], P('gx', 'gy', 'gz'), may hold values from 0 to 1, as said below
- counts: int32 [8, 4, 8], P('gx', 'gy', 'gz'), may hold values from 1 to 128, as said below
Outputs:
- acceleration: float32 [8, 4, 8, 3, 128], P('gx', 'gy', 'gz')
- energy_rate: float32 [8, 4, 8, 128], P('gx', 'gy', 'gz')
The draws below stay inside these ranges and needn't reach their ends.
Inputs may be any that keep to these rules, and one draw needn't show every extreme that they name: `partner_mask`: partner 13 (the leaf itself) is always 1. `counts`: some leaf holds 128 valid particles.
All inputs are finite; a program needn't handle non-finite values.
Results may differ from the reference program's by a relative error of at most 0.0003.
Values sent between devices are 32-bit elements; how exact they have to be, the bound alone decides.
No kernel may reach another device: no remote copies, remote signals or barrier semaphores. Data moves between devices by JAX's collectives and lax.ppermute only.
A program may use at most 64 MiB of HBM per device.

```python
import math
import jax
import jax.numpy as jnp
from jax import lax

P_SIZE = 128
LX = 2
LY = 2
LZ = 2
NLX = 8
NLY = 4
NLZ = 8


def draw_partner_mask(key, part):
    picks = jax.random.randint(key, (NLX, NLY, NLZ, 27), 0, 5)
    own = jnp.arange(27, dtype=jnp.int32) == 13
    kept = (picks < 4).astype(jnp.int32)
    return jnp.where(own[None, None, None, :], 1, kept).astype(jnp.int32)


def draw_counts(key, part):
    first = jax.random.fold_in(key, 11)
    second = jax.random.fold_in(key, 23)
    level = jax.random.randint(first, (NLX // LX, NLY // LY, NLZ // LZ), 0, 4)
    level = jnp.repeat(jnp.repeat(jnp.repeat(level, LX, 0), LY, 1), LZ, 2)
    ceiling = P_SIZE // jnp.left_shift(jnp.ones_like(level), level)
    drawn = 1 + jax.random.randint(second, level.shape, 0, ceiling)
    drawn = drawn.at[0, 0, 0].set(P_SIZE)
    return drawn.astype(jnp.int32)


def block_scale(stream_key, dims, pieces, least, largest):
    level, own = 1.0, jax.random.fold_in(stream_key, 6)
    for position, parts in pieces:
        heights = jnp.exp(jax.random.uniform(jax.random.fold_in(own, position), (parts,), jnp.float32, least / len(pieces), largest / len(pieces)))
        level = level * jnp.repeat(heights, dims[position] // parts).reshape([-1 if axis == position else 1 for axis in range(len(dims))])
    return level


def normal_values(key, dims, spread, bound, shards=(), kind=jnp.bfloat16):
    array = jax.random.normal(key, dims, jnp.float32) * spread
    if len(shards) > 0:
        array = block_scale(key, dims, shards, -0.22, 0.18) * array
    return jnp.clip(array, min=-bound, max=bound).astype(kind)


def setup_inputs(seed: int = 0) -> dict:
    splits = jax.random.split(jax.random.key(seed), 7)
    offsets = jnp.clip(1.0 * jax.random.uniform(splits[0], (NLX, NLY, NLZ, 3, P_SIZE), jnp.float32) ** block_scale(splits[0], (NLX, NLY, NLZ, 3, P_SIZE), ((0, 4), (1, 2), (2, 4)), -0.2, 0.2), 0.0, 1.0)
    velocity = normal_values(splits[1], (NLX, NLY, NLZ, 3, P_SIZE), 1.0, 6.0, ((0, 4), (1, 2), (2, 4)), jnp.float32)
    mass = jnp.clip(jnp.exp(math.log(0.2) - 1.3862944 * jax.random.uniform(splits[2], (NLX, NLY, NLZ, P_SIZE), jnp.float32) ** block_scale(splits[2], (NLX, NLY, NLZ, P_SIZE), ((0, 4), (1, 2), (2, 4)), -0.2, 0.2)), 0.05, 0.2)
    energy = jnp.clip(jnp.exp(math.log(2.0) - 1.3862944 * jax.random.uniform(splits[3], (NLX, NLY, NLZ, P_SIZE), jnp.float32) ** block_scale(splits[3], (NLX, NLY, NLZ, P_SIZE), ((0, 4), (1, 2), (2, 4)), -0.2, 0.2)), 0.5, 2.0)
    partner_mask = draw_partner_mask(jax.random.fold_in(splits[6], 71), 0)
    counts = draw_counts(jax.random.fold_in(splits[6], 71), 0)
    return {"offsets": offsets, "velocity": velocity, "mass": mass, "energy": energy, "partner_mask": partner_mask, "counts": counts}


def pair_geometry(center, partner, shift):
    separation = center[:, :, 0:3, :, None] - partner[:, :, 0:3, None, :] - shift[None, None, :, None, None]
    radius = jnp.sqrt(lax.optimization_barrier(jnp.sum(separation * separation, axis=2)))
    inside = jnp.maximum(1.0 - radius, 0.0)
    cubed = inside * inside * inside
    kernel = cubed * inside * (1.0 + 4.0 * radius)
    slope = -20.0 * cubed
    return (separation, kernel, slope)

def volume_terms(center, partner, shift):
    separation, kernel, slope = pair_geometry(center, partner, shift)
    return lax.optimization_barrier(jnp.sum(kernel * partner[:, :, 3, None, :], axis=-1))[:, :, None, :]

def density_terms(center, partner, shift):
    separation, kernel, slope = pair_geometry(center, partner, shift)
    weight = partner[:, :, 3, None, :]
    mass_far = partner[:, :, 4, None, :]
    volume_far = partner[:, :, 8, None, :]
    summed_mass = lax.optimization_barrier(jnp.sum(weight * mass_far * kernel, axis=-1))
    summed_volume = lax.optimization_barrier(jnp.sum(weight * volume_far * kernel, axis=-1))
    relative = lax.optimization_barrier(jnp.sum((partner[:, :, 5:8, None, :] - center[:, :, 5:8, :, None]) * separation, axis=2))
    divergence = lax.optimization_barrier(jnp.sum(weight * volume_far * slope * relative, axis=-1))
    return jnp.stack([summed_mass, summed_volume, divergence], axis=2)

def force_terms(center, partner, shift):
    separation, kernel, slope = pair_geometry(center, partner, shift)
    weight = partner[:, :, 3, None, :]
    mass_far = partner[:, :, 4, None, :]
    dens_own = center[:, :, 9, :, None]
    dens_far = partner[:, :, 9, None, :]
    specific_own = center[:, :, 10, :, None] / (dens_own * dens_own)
    specific_far = partner[:, :, 10, None, :] / (dens_far * dens_far)
    visc_own = jnp.maximum(-center[:, :, 11, :, None], 0.0)
    visc_far = jnp.maximum(-partner[:, :, 11, None, :], 0.0)
    damping = 2.0 * (visc_own + visc_far) / (dens_own + dens_far)
    scaled = weight * mass_far * slope
    push = scaled * (specific_own + specific_far + damping)
    accel = -lax.optimization_barrier(jnp.sum(push[:, :, None] * separation, axis=-1))
    closing = lax.optimization_barrier(jnp.sum((center[:, :, 5:8, :, None] - partner[:, :, 5:8, None, :]) * separation, axis=2))
    heating = lax.optimization_barrier(jnp.sum(scaled * (specific_own + 0.5 * damping) * closing, axis=-1))
    return jnp.concatenate([accel, heating[:, :, None, :]], axis=2)

def sweep(padded, mask, terms_fn, width_out):
    rows = padded.shape[0] - 2
    cols = padded.shape[1] - 2
    depth = padded.shape[2] - 2
    chans = padded.shape[3]
    slots = padded.shape[4]
    zero = jnp.zeros((), jnp.int32)

    def leaf_row(index):
        slab = lax.dynamic_slice_in_dim(padded, index, 3, 0)
        center = slab[1, 1:-1, 1:-1]
        row_mask = None
        if mask is not None:
            row_mask = lax.dynamic_index_in_dim(mask, index, 0, keepdims=False).astype(jnp.float32)

        def partner_step(partner, total):
            off_x = partner // 9
            off_y = partner // 3 % 3
            off_z = partner % 3
            neighbour = lax.dynamic_slice(slab, (off_x, off_y, off_z, zero, zero), (1, cols, depth, chans, slots))[0]
            shift = jnp.stack([off_x, off_y, off_z]).astype(jnp.float32) - 1.0
            terms = terms_fn(center, neighbour, shift)
            if row_mask is not None:
                picked = lax.dynamic_index_in_dim(row_mask, partner, 2, keepdims=False)
                terms = terms * picked[:, :, None, None]
            return total + terms
        start = jnp.zeros((cols, depth, width_out, slots), jnp.float32)
        return lax.fori_loop(jnp.int32(0), jnp.int32(27), partner_step, start)
    return lax.map(leaf_row, jnp.arange(rows, dtype=jnp.int32))

def wrapped(field):
    return jnp.pad(field, ((1, 1), (1, 1), (1, 1), (0, 0), (0, 0)), mode='wrap')

def reference(offsets, velocity, mass, energy, partner_mask, counts):
    slot_ids = jnp.arange(P_SIZE, dtype=jnp.int32)
    valid = (slot_ids[None, None, None, :] < counts[:, :, :, None]).astype(jnp.float32)
    base = jnp.concatenate([offsets, valid[:, :, :, None], mass[:, :, :, None], velocity], axis=3)
    volume = 1.0 / (1.0 + sweep(wrapped(base[:, :, :, 0:4]), None, volume_terms, 1)[:, :, :, 0])
    second = jnp.concatenate([base, volume[:, :, :, None]], axis=3)
    summed = sweep(wrapped(second), partner_mask, density_terms, 3)
    density = (mass + summed[:, :, :, 0]) / (volume + summed[:, :, :, 1])
    divergence = summed[:, :, :, 2]
    pressure = 2.0 / 3.0 * density * energy
    state = jnp.stack([density, pressure, divergence], axis=3)
    third = jnp.concatenate([second, state], axis=3)
    forces = sweep(wrapped(third), partner_mask, force_terms, 4)
    acceleration = forces[:, :, :, 0:3] * valid[:, :, :, None]
    energy_rate = forces[:, :, :, 3] * valid
    return (acceleration, energy_rate)
```

```python
import functools
import itertools

import jax
import jax.numpy as jnp
from jax import lax
from jax.experimental import pallas as pl
from jax.experimental.pallas import tpu as pltpu
from jax.sharding import PartitionSpec as P

AXES = (("gx", 0), ("gy", 1), ("gz", 2))
FAR = 1024.0
TINY = 1e-30
GROUP = 4
OFFSETS = tuple(itertools.product((-1, 0, 1), repeat=3))


def extended(block, sides):
    for axis, dim in sides:
        count = lax.axis_size(axis)
        size = block.shape[dim]
        last = lax.slice_in_dim(block, size - 1, None, axis=dim)
        first = lax.slice_in_dim(block, 0, 1, axis=dim)
        if count == 1:
            low, high = last, first
        elif count == 2:
            ends = block if size == 2 else jnp.concatenate([first, last], axis=dim)
            ends = lax.ppermute(ends, axis, [(0, 1), (1, 0)])
            low = lax.slice_in_dim(ends, 1, 2, axis=dim)
            high = lax.slice_in_dim(ends, 0, 1, axis=dim)
        else:
            forward = [(i, (i + 1) % count) for i in range(count)]
            backward = [(target, source) for source, target in forward]
            low = lax.ppermute(last, axis, forward)
            high = lax.ppermute(first, axis, backward)
        block = jnp.concatenate([low, block, high], axis=dim)
    return block


def column_constant(values, rows):
    ids = lax.broadcasted_iota(jnp.int32, (rows, 128), 0)
    out = jnp.zeros((rows, 128), jnp.float32)
    for row, value in enumerate(values):
        if value != 0.0:
            out = jnp.where(ids == row, jnp.float32(value), out)
    return out


def pair_inside(own, row):
    dx = own[0] - row(0)
    dy = own[1] - row(1)
    dz = own[2] - row(2)
    square = dx * dx + dy * dy + dz * dz
    radius = square * lax.rsqrt(jnp.maximum(square, TINY))
    return dx, dy, dz, jnp.maximum(1.0 - radius, 0.0)


def kernel_value(inside):
    second = inside * inside
    return second * second * (5.0 - 4.0 * inside)


def volume_pair(own, row, sums):
    _, _, _, inside = pair_inside(own, row)
    return (sums[0] + kernel_value(inside),)


def density_pair(own, row, sums):
    dx, dy, dz, inside = pair_inside(own, row)
    second = inside * inside
    value = second * second * (5.0 - 4.0 * inside)
    mass, volume = row(3), row(7)
    relative = (row(4) - own[4]) * dx + (row(5) - own[5]) * dy + (row(6) - own[6]) * dz
    return (
        sums[0] + mass * value,
        sums[1] + volume * value,
        sums[2] + volume * (second * inside) * relative,
    )


def force_pair(own, row, sums):
    dx, dy, dz, inside = pair_inside(own, row)
    scaled = row(3) * (inside * inside * inside)
    relative = (own[4] - row(4)) * dx + (own[5] - row(5)) * dy + (own[6] - row(6)) * dz
    half = (own[10] + row(10)) / (own[8] + row(8))
    heat = own[9] + half
    push = (heat + (row(9) + half)) * scaled
    return (
        sums[0] + push * dx,
        sums[1] + push * dy,
        sums[2] + push * dz,
        sums[3] + heat * scaled * relative,
    )


def sweep_kernel(
    grid, rows_own, n_sums, pair, finish, masked, tail, counts_ref, mask_ref, near_ref, own_ref, out_ref, list_ref, col_ref, sum_ref
):
    nx, ny, nz = grid
    height = near_ref.shape[1]
    slots = near_ref.shape[2]
    lanes = lax.broadcasted_iota(jnp.int32, (height, slots), 1)
    out_lanes = lax.broadcasted_iota(jnp.int32, (8, slots), 1)
    far = column_constant(tail, height)
    span = (ny + 2) * (nz + 2)

    def leaf_step(leaf, carry):
        lx = leaf // (ny * nz)
        ly = leaf // nz % ny
        lz = leaf % nz
        home = (lx + 1) * span + (ly + 1) * (nz + 2) + (lz + 1)

        start = jnp.int32(0)
        held = far
        for k, (ox, oy, oz) in enumerate(OFFSETS):
            place = home + (ox * span + oy * (nz + 2) + oz)
            block = near_ref[place]
            if (ox, oy, oz) != (0, 0, 0):
                block = block + column_constant((ox, oy, oz), height)
            shift = start % slots
            tile = start // slots
            rolled = pltpu.roll(block, shift, axis=1)
            held = jnp.where(lanes >= shift, rolled, held)
            list_ref[tile] = held
            list_ref[tile + 1] = rolled
            size = counts_ref[place]
            if masked:
                size = size * mask_ref[leaf * 27 + k]
            start = start + size
            held = jnp.where(start // slots > tile, rolled, held)
        tile = start // slots
        list_ref[tile] = jnp.where(lanes >= start % slots, far, held)
        steps = (start + (slots - 1)) // slots

        count = counts_ref[home]
        center = near_ref[home]
        full = jnp.concatenate([center, jnp.zeros((slots - height, slots), jnp.float32)], axis=0)
        col_ref[...] = jnp.transpose(full)

        def group_step(group, carry):
            owns = []
            for part in range(GROUP):
                at = pl.multiple_of(group * (8 * GROUP) + 8 * part, 8)
                cols = col_ref[pl.ds(at, 8), :]
                owns.append(
                    {c: jnp.broadcast_to(cols[:, c : c + 1], (8, slots)) for c in rows_own}
                )

            def partner_step(step, sums):
                rows = {}

                def row(c):
                    if c not in rows:
                        rows[c] = jnp.broadcast_to(list_ref[step, c : c + 1, :], (8, slots))
                    return rows[c]

                return tuple(pair(owns[part], row, sums[part]) for part in range(GROUP))

            zero = jnp.zeros((8, slots), jnp.float32)
            sums = lax.fori_loop(0, steps, partner_step, tuple((zero,) * n_sums for _ in range(GROUP)))
            for part in range(GROUP):
                at = pl.multiple_of(group * (8 * GROUP) + 8 * part, 8)
                packed = zero
                for index in range(n_sums):
                    total = jnp.sum(sums[part][index], axis=1, keepdims=True)
                    packed = jnp.where(out_lanes == index, total, packed)
                sum_ref[pl.ds(at, 8), :] = packed
            return carry

        lax.fori_loop(0, (count + 8 * GROUP - 1) // (8 * GROUP), group_step, 0)
        sums = jnp.transpose(sum_ref[...])
        valid = lax.broadcasted_iota(jnp.int32, (1, slots), 1) < count
        finish(leaf, [sums[i : i + 1] for i in range(n_sums)], valid, center, own_ref, out_ref)
        return carry

    lax.fori_loop(0, nx * ny * nz, leaf_step, 0)


def volume_finish(leaf, sums, valid, center, own_ref, out_ref):
    out_ref[leaf, 0:1, :] = jnp.where(valid, 1.0 / (1.0 + sums[0]), 1.0)


def density_finish(leaf, sums, valid, center, own_ref, out_ref):
    density = (center[3:4] + sums[0]) / (center[7:8] + sums[1])
    density = jnp.where(valid, density, 1.0)
    out_ref[leaf, 0:1, :] = density
    out_ref[leaf, 1:2, :] = jnp.where(valid, (2.0 / 3.0) * own_ref[leaf, 0:1, :] / density, 0.0)
    out_ref[leaf, 2:3, :] = jnp.where(valid, jnp.maximum(20.0 * sums[2], 0.0), 0.0)


def force_finish(leaf, sums, valid, center, own_ref, out_ref):
    for index in range(3):
        out_ref[leaf, index : index + 1, :] = jnp.where(valid, 20.0 * sums[index], 0.0)
    out_ref[leaf, 3:4, :] = jnp.where(valid, -20.0 * sums[3], 0.0)


def sweep(near, counts, mask, own, grid, rows_own, n_sums, n_out, pair, finish, masked, tail):
    height, slots = near.shape[1:]
    leaves = grid[0] * grid[1] * grid[2]
    body = functools.partial(sweep_kernel, grid, rows_own, n_sums, pair, finish, masked, tail)
    return pl.pallas_call(
        body,
        out_shape=jax.ShapeDtypeStruct((leaves, n_out, slots), jnp.float32),
        in_specs=[
            pl.BlockSpec(memory_space=pltpu.SMEM),
            pl.BlockSpec(memory_space=pltpu.SMEM),
            pl.BlockSpec(memory_space=pltpu.VMEM),
            pl.BlockSpec(memory_space=pltpu.VMEM),
        ],
        out_specs=pl.BlockSpec(memory_space=pltpu.VMEM),
        scratch_shapes=[
            pltpu.VMEM((30, height, slots), jnp.float32),
            pltpu.VMEM((slots, slots), jnp.float32),
            pltpu.VMEM((slots, slots), jnp.float32),
        ],
        name=pair.__name__,
    )(counts, mask, near, own)


def flat(block):
    return block.reshape((-1,) + block.shape[3:])


def shards(offsets, velocity, mass, energy, partner_mask, counts):
    grid = counts.shape
    slots = offsets.shape[4]
    number = jnp.broadcast_to(counts.astype(jnp.float32)[..., None, None], grid + (1, slots))
    places = extended(jnp.concatenate([offsets, number], axis=3), AXES)
    near_counts = places[:, :, :, 3, 0].astype(jnp.int32).reshape(-1)
    mask = partner_mask.reshape(-1)
    own_energy = energy.reshape((-1, 1, slots))

    volume = sweep(
        flat(places), near_counts, mask, own_energy, grid, (0, 1, 2), 1, 1,
        volume_pair, volume_finish, False, (FAR, FAR, FAR),
    ).reshape(grid + (1, slots))

    carried = extended(jnp.concatenate([mass[:, :, :, None], velocity, volume], axis=3), AXES)
    second = jnp.concatenate([places[:, :, :, 0:3], carried], axis=3)
    state = sweep(
        flat(second), near_counts, mask, own_energy, grid, (0, 1, 2, 4, 5, 6), 3, 3,
        density_pair, density_finish, True, (FAR, FAR, FAR),
    ).reshape(grid + (3, slots))

    around = extended(state, AXES)
    spare = jnp.zeros(around.shape[:3] + (5, slots), jnp.float32)
    third = jnp.concatenate([second, around, spare], axis=3)
    forces = sweep(
        flat(third), near_counts, mask, own_energy, grid, (0, 1, 2, 4, 5, 6, 8, 9, 10), 4, 4,
        force_pair, force_finish, True, (FAR, FAR, FAR, 0.0, 0.0, 0.0, 0.0, 0.0, 1.0),
    ).reshape(grid + (4, slots))
    return forces[:, :, :, 0:3], forces[:, :, :, 3]


def solution(mesh):
    placed = (
        P("gx", "gy", "gz", None, None),
        P("gx", "gy", "gz", None, None),
        P("gx", "gy", "gz", None),
        P("gx", "gy", "gz", None),
        P("gx", "gy", "gz", None),
        P("gx", "gy", "gz"),
    )
    return jax.shard_map(
        shards,
        mesh=mesh,
        in_specs=placed,
        out_specs=(P("gx", "gy", "gz", None, None), P("gx", "gy", "gz", None)),
        check_vma=False,
    )
```

```python
import functools
import itertools

import jax
import jax.numpy as jnp
from jax import lax
from jax.experimental import pallas as pl
from jax.experimental.pallas import tpu as pltpu
from jax.sharding import PartitionSpec as P

AXES = (("gx", 0), ("gy", 1), ("gz", 2))
FAR = 1024.0
TINY = 1e-30
ROOM = 6 << 20
GROUP = 4
AHEAD = 2
WIDE = (0, 1, 2, 4, 5, 6)
OFFSETS = tuple(itertools.product((-1, 0, 1), repeat=3))


def extended(block, sides):
    for axis, dim in sides:
        count = lax.axis_size(axis)
        size = block.shape[dim]
        last = lax.slice_in_dim(block, size - 1, None, axis=dim)
        first = lax.slice_in_dim(block, 0, 1, axis=dim)
        if count == 1:
            low, high = last, first
        elif count == 2:
            ends = block if size == 2 else jnp.concatenate([first, last], axis=dim)
            ends = lax.ppermute(ends, axis, [(0, 1), (1, 0)])
            low = lax.slice_in_dim(ends, 1, 2, axis=dim)
            high = lax.slice_in_dim(ends, 0, 1, axis=dim)
        else:
            forward = [(i, (i + 1) % count) for i in range(count)]
            backward = [(target, source) for source, target in forward]
            low = lax.ppermute(last, axis, forward)
            high = lax.ppermute(first, axis, backward)
        block = jnp.concatenate([low, block, high], axis=dim)
    return block


def column_constant(values, rows):
    ids = lax.broadcasted_iota(jnp.int32, (rows, 128), 0)
    out = jnp.zeros((rows, 128), jnp.float32)
    for row, value in enumerate(values):
        if value != 0.0:
            out = jnp.where(ids == row, jnp.float32(value), out)
    return out


def pair_inside(own, row):
    dx = own[0] - row(0)
    dy = own[1] - row(1)
    dz = own[2] - row(2)
    square = dx * dx + dy * dy + dz * dz
    radius = square * lax.rsqrt(jnp.maximum(square, TINY))
    return dx, dy, dz, jnp.maximum(1.0 - radius, 0.0)


def volume_pair(own, row):
    _, _, _, inside = pair_inside(own, row)
    second = inside * inside
    return ((second * second) * (1.25 - inside),)


def density_pair(own, row):
    dx, dy, dz, inside = pair_inside(own, row)
    third = inside * inside * inside
    value = third * (inside * (1.25 - inside))
    relative = (row(4) - own[4]) * dx + (row(5) - own[5]) * dy + (row(6) - own[6]) * dz
    volume = row(7)
    return (
        row(3) * value,
        volume * value,
        (volume * third) * relative,
    )


def force_pair(own, row):
    dx, dy, dz, inside = pair_inside(own, row)
    scaled = row(3) * (inside * inside * inside)
    relative = (own[4] - row(4)) * dx + (own[5] - row(5)) * dy + (own[6] - row(6)) * dz
    half = (own[10] + row(10)) / (own[8] + row(8))
    heat = own[9] + half
    push = (heat + (row(9) + half)) * scaled
    return (
        push * dx,
        push * dy,
        push * dz,
        (heat * scaled) * relative,
    )


def prepare_kernel(counts_hbm, offsets_hbm, velocity_hbm, mass_hbm, out_ref, *scratch):
    sources = (counts_hbm, offsets_hbm, velocity_hbm, mass_hbm)
    holds, sems = scratch[:4], scratch[4]
    copies = [
        pltpu.make_async_copy(source, hold, sems.at[i])
        for i, (source, hold) in enumerate(zip(sources, holds))
    ]
    for copy in copies:
        copy.start()
    for copy in copies:
        copy.wait()
    counts_ref, offsets_ref, velocity_ref, mass_ref = holds
    nx, ny, nz = mass_ref.shape[:3]
    for leaf, (x, y, z) in enumerate(itertools.product(range(nx), range(ny), range(nz))):
        for c in range(3):
            out_ref[leaf, c : c + 1, :] = offsets_ref[x, y, c, z : z + 1, :]
            out_ref[leaf, 4 + c : 5 + c, :] = velocity_ref[x, y, c, z : z + 1, :]
        out_ref[leaf, 3:4, :] = mass_ref[x, y, z : z + 1, :]
        number = counts_ref[x, y : y + 1, z : z + 1].astype(jnp.float32)
        out_ref[leaf, 7:8, :] = jnp.broadcast_to(number, (1, mass_ref.shape[3]))


def homes(grid):
    nx, ny, nz = grid
    span = (ny + 2) * (nz + 2)
    places = [
        (x + 1) * span + (y + 1) * (nz + 2) + z + 1
        for x, y, z in itertools.product(range(nx), range(ny), range(nz))
    ]
    return places, [ox * span + oy * (nz + 2) + oz for ox, oy, oz in OFFSETS]


def split_place(start):
    return start & 127, lax.shift_right_logical(start, 7)


def put(list_ref, leaf, shift, tile, block, lanes):
    rolled = pltpu.roll(block, shift, axis=1)
    pltpu.store(list_ref.at[leaf, tile], rolled, mask=lanes >= shift)
    list_ref[leaf, tile + 1] = rolled


def close(list_ref, leaf, shift, tile, tail, lanes):
    pltpu.store(list_ref.at[leaf, tile], tail, mask=lanes >= shift)
    for step in range(1, AHEAD):
        list_ref[leaf, tile + step] = tail


def lane_ids(rows):
    return lax.broadcasted_iota(jnp.int32, (rows, 128), 1)


def pack_places(grid, near_ref, list_ref, size_of, note):
    lanes = lane_ids(8)
    far = column_constant((FAR, FAR, FAR), 8)
    shifts = [column_constant(offset, 8) for offset in OFFSETS]
    places, steps = homes(grid)
    for leaf, home in enumerate(places):
        start = jnp.int32(0)
        for k, step in enumerate(steps):
            shift, tile = split_place(start)
            note(leaf, k, shift, tile)
            put(list_ref, leaf, shift, tile, near_ref[home + step] + shifts[k], lanes)
            start = start + size_of(leaf, k, home + step)
        shift, tile = split_place(start)
        note(leaf, 27, shift, tile)
        close(list_ref, leaf, shift, tile, far, lanes)


def pack_side(grid, more_ref, side_ref, shift_ref, tile_ref, tail):
    height = more_ref.shape[1]
    lanes = lane_ids(height)
    last = column_constant(tail, height)
    places, steps = homes(grid)
    for leaf, home in enumerate(places):
        for k, step in enumerate(steps):
            at = leaf * 28 + k
            put(side_ref, leaf, shift_ref[at], tile_ref[at], more_ref[home + step], lanes)
        at = leaf * 28 + 27
        close(side_ref, leaf, shift_ref[at], tile_ref[at], last, lanes)


def widen_kernel(rows, block_ref, out_ref):
    for leaf in range(block_ref.shape[0]):
        for index, c in enumerate(rows):
            row = block_ref[leaf, c : c + 1, :]
            out_ref[leaf, index] = jnp.transpose(jnp.broadcast_to(row, (128, 128)))


def arrange_kernel(grid, counts_ref, mask_ref, near_ref, list_ref, shift_ref, tile_ref):
    def size_of(leaf, k, place):
        return counts_ref[place] * mask_ref[leaf * 27 + k]

    def note(leaf, k, shift, tile):
        shift_ref[leaf * 28 + k] = shift
        tile_ref[leaf * 28 + k] = tile

    pack_places(grid, near_ref, list_ref, size_of, note)


def run_pairs(grid, pair, n_sums, count_of, tiles_of, own_of, row_of, finish, acc_ref):
    nx, ny, nz = grid
    span = (ny + 2) * (nz + 2)
    zero = jnp.zeros((8, 128), jnp.float32)

    def leaf_step(lx, ly, lz):
        leaf = (lx * ny + ly) * nz + lz
        home = (lx + 1) * span + (ly + 1) * (nz + 2) + (lz + 1)
        count = count_of(home)
        steps = lax.shift_right_logical(tiles_of(leaf) + AHEAD, AHEAD.bit_length() - 1)

        def group_step(group, carry):
            places = [
                pl.ds(pl.multiple_of(group * (8 * GROUP) + 8 * part, 8), 8) for part in range(GROUP)
            ]
            owns = [own_of(leaf, at) for at in places]

            def partner_step(step, sums):
                for more in range(AHEAD):
                    rows = {}
                    at = step * AHEAD + more

                    def row(c):
                        if c not in rows:
                            rows[c] = jnp.broadcast_to(row_of(leaf, at, c), (8, 128))
                        return rows[c]

                    terms = [pair(own, row) for own in owns]
                    sums = tuple(
                        tuple(a + b for a, b in zip(old, new)) for old, new in zip(sums, terms)
                    )
                return sums

            sums = lax.fori_loop(0, steps, partner_step, ((zero,) * n_sums,) * GROUP)
            for part, at in enumerate(places):
                for index in range(n_sums):
                    acc_ref[index, at, :] = sums[part][index]
            return carry

        groups = lax.shift_right_logical(count + (8 * GROUP - 1), (8 * GROUP).bit_length() - 1)
        lax.fori_loop(0, groups, group_step, 0)
        valid = lax.broadcasted_iota(jnp.int32, (1, 128), 1) < count
        sums = [jnp.sum(jnp.transpose(acc_ref[i]), axis=0, keepdims=True) for i in range(n_sums)]
        finish((lx, ly, lz), leaf, sums, valid)

    def x_step(lx, carry):
        def y_step(ly, carry):
            def z_step(lz, carry):
                leaf_step(lx, ly, lz)
                return carry

            return lax.fori_loop(0, nz, z_step, carry)

        return lax.fori_loop(0, ny, y_step, carry)

    lax.fori_loop(0, nx, x_step, 0)


def own_reader(*pieces):
    def own_of(leaf, at):
        return {c: ref[leaf, i, at, :] for ref, channels in pieces for i, c in enumerate(channels)}

    return own_of


def row_reader(list_ref, side_ref=None, base=8):
    def row_of(leaf, at, c):
        if c < base:
            return list_ref[leaf, at, c : c + 1, :]
        return side_ref[leaf, at, c - base : c - base + 1, :]

    return row_of


def volume_kernel(grid, near_ref, wide_ref, out_ref, counts_ref, list_ref, acc_ref, last_ref):
    for place in range(near_ref.shape[0]):
        counts_ref[place] = near_ref[place, 7:8, :].astype(jnp.int32)[0, 0]

    def note(leaf, k, shift, tile):
        if k == 27:
            last_ref[leaf] = tile

    pack_places(grid, near_ref, list_ref, lambda leaf, k, place: counts_ref[place], note)

    def finish(index, leaf, sums, valid):
        out_ref[leaf] = jnp.where(valid, 1.0 / (1.0 + 4.0 * sums[0]), 1.0)

    run_pairs(
        grid, volume_pair, 1, lambda home: counts_ref[home], lambda leaf: last_ref[leaf],
        own_reader((wide_ref, WIDE)), row_reader(list_ref), finish, acc_ref,
    )


def density_kernel(
    grid, counts_ref, shift_ref, tile_ref, list_ref, wide_ref, more_ref, own_ref, volume_ref, energy_ref,
    out_ref, side_ref, acc_ref,
):
    pack_side(grid, more_ref, side_ref, shift_ref, tile_ref, ())

    def finish(index, leaf, sums, valid):
        lx, ly, lz = index
        density = (own_ref[leaf, 3:4, :] + 4.0 * sums[0]) / (volume_ref[leaf] + 4.0 * sums[1])
        density = jnp.where(valid, density, 1.0)
        energy = energy_ref[lx, ly, pl.ds(lz, 1), :]
        out_ref[leaf, 0:1, :] = density
        out_ref[leaf, 1:2, :] = jnp.where(valid, (2.0 / 3.0) * energy / density, 0.0)
        out_ref[leaf, 2:3, :] = jnp.where(valid, jnp.maximum(20.0 * sums[2], 0.0), 0.0)
        out_ref[leaf, 3:4, :] = jnp.zeros_like(density)

    run_pairs(
        grid, density_pair, 3, lambda home: counts_ref[home], lambda leaf: tile_ref[leaf * 28 + 27],
        own_reader((wide_ref, WIDE)), row_reader(list_ref, side_ref, 7), finish, acc_ref,
    )


def force_kernel(
    grid, counts_ref, shift_ref, tile_ref, list_ref, wide_ref, state_ref, more_ref,
    push_ref, heat_ref, side_ref, acc_ref,
):
    pack_side(grid, more_ref, side_ref, shift_ref, tile_ref, (1.0,))

    def finish(index, leaf, sums, valid):
        lx, ly, lz = index
        for c in range(3):
            push_ref[lx, ly, c, pl.ds(lz, 1), :] = jnp.where(valid, 20.0 * sums[c], 0.0)
        heat_ref[lx, ly, pl.ds(lz, 1), :] = jnp.where(valid, -20.0 * sums[3], 0.0)

    run_pairs(
        grid, force_pair, 4, lambda home: counts_ref[home], lambda leaf: tile_ref[leaf * 28 + 27],
        own_reader((wide_ref, WIDE), (state_ref, (8, 9, 10))), row_reader(list_ref, side_ref), finish, acc_ref,
    )


def call(name, body, inputs, outs, scratch=(), cycles=0):
    def spec(x):
        scalar = x.dtype == jnp.int32 and len(x.shape) == 1
        return pl.BlockSpec(memory_space=pltpu.SMEM if scalar else pltpu.VMEM)

    return pl.pallas_call(
        body,
        out_shape=outs,
        in_specs=[spec(x) for x in inputs],
        out_specs=[spec(x) for x in outs],
        scratch_shapes=scratch,
        compiler_params=pltpu.CompilerParams(vmem_limit_bytes=ROOM),
        cost_estimate=pl.CostEstimate(flops=cycles * 4096, bytes_accessed=1 << 20, transcendentals=0),
        name=name,
    )(*inputs)


def floats(*shape):
    return jax.ShapeDtypeStruct(shape, jnp.float32)


def integers(*shape):
    return jax.ShapeDtypeStruct(shape, jnp.int32)


def flat(block):
    return block.reshape((-1,) + block.shape[3:])


def shards(offsets, velocity, mass, energy, partner_mask, counts):
    grid = counts.shape
    slots = offsets.shape[4]
    assert slots == 128
    leaves = grid[0] * grid[1] * grid[2]
    tiles = 27 + 1 + AHEAD
    inputs = (counts, jnp.swapaxes(offsets, 2, 3), jnp.swapaxes(velocity, 2, 3), mass)
    own = pl.pallas_call(
        prepare_kernel,
        out_shape=floats(leaves, 8, slots),
        in_specs=[pl.BlockSpec(memory_space=pltpu.HBM)] * 4,
        out_specs=pl.BlockSpec(memory_space=pltpu.VMEM),
        scratch_shapes=[pltpu.VMEM(x.shape, x.dtype) for x in inputs] + [pltpu.SemaphoreType.DMA((4,))],
        compiler_params=pltpu.CompilerParams(vmem_limit_bytes=ROOM),
        name="prepare",
    )(*inputs)
    mask = partner_mask.reshape(-1)
    near = flat(extended(own.reshape(grid + (8, slots)), AXES))
    wide = call(
        "widen", functools.partial(widen_kernel, WIDE), [own],
        [floats(leaves, len(WIDE), slots, slots)], cycles=2000,
    )[0]

    volume, near_counts = call(
        "volume", functools.partial(volume_kernel, grid), [near, wide],
        [floats(leaves, 1, slots), integers(near.shape[0])],
        [
            pltpu.VMEM((leaves, tiles, 8, slots), jnp.float32),
            pltpu.VMEM((1, slots, slots), jnp.float32),
            pltpu.SMEM((leaves,), jnp.int32),
        ],
        cycles=6000,
    )
    near_volume = flat(extended(volume.reshape(grid + (1, slots)), AXES))
    lists, shifts, starts = call(
        "arrange", functools.partial(arrange_kernel, grid), [near_counts, mask, near],
        [floats(leaves, tiles, 8, slots), integers(leaves * 28), integers(leaves * 28)], cycles=1500,
    )

    state = call(
        "density", functools.partial(density_kernel, grid),
        [near_counts, shifts, starts, lists, wide, near_volume, own, volume, energy],
        [floats(leaves, 4, slots)],
        [
            pltpu.VMEM((leaves, tiles, 1, slots), jnp.float32),
            pltpu.VMEM((3, slots, slots), jnp.float32),
        ],
        cycles=8000,
    )[0]
    near_state = flat(extended(state.reshape(grid + (4, slots)), AXES))
    wide_state = call(
        "widen_state", functools.partial(widen_kernel, (0, 1, 2)), [state],
        [floats(leaves, 3, slots, slots)], cycles=1000,
    )[0]

    push, heat = call(
        "force", functools.partial(force_kernel, grid),
        [near_counts, shifts, starts, lists, wide, wide_state, near_state],
        [floats(*grid[:2], 3, grid[2], slots), floats(*grid, slots)],
        [
            pltpu.VMEM((leaves, tiles, 4, slots), jnp.float32),
            pltpu.VMEM((4, slots, slots), jnp.float32),
        ],
        cycles=10000,
    )
    return jnp.swapaxes(push, 2, 3), heat


def solution(mesh):
    placed = (
        P("gx", "gy", "gz", None, None),
        P("gx", "gy", "gz", None, None),
        P("gx", "gy", "gz", None),
        P("gx", "gy", "gz", None),
        P("gx", "gy", "gz", None),
        P("gx", "gy", "gz"),
    )
    return jax.shard_map(
        shards,
        mesh=mesh,
        in_specs=placed,
        out_specs=(P("gx", "gy", "gz", None, None), P("gx", "gy", "gz", None)),
        check_vma=False,
    )
```

```python
import functools
import itertools

import jax
import jax.numpy as jnp
from jax import lax
from jax.experimental import pallas as pl
from jax.experimental.pallas import tpu as pltpu
from jax.sharding import PartitionSpec as P

AXES = (("gx", 0), ("gy", 1), ("gz", 2))
FAR = 1024.0
TINY = 1e-30
ROOM = 6 << 20
GROUP = 4
AHEAD = 2
WIDE = (0, 1, 2, 4, 5, 6)
OFFSETS = tuple(itertools.product((-1, 0, 1), repeat=3))


def ends_of(block, axis, dim):
    count = lax.axis_size(axis)
    size = block.shape[dim]
    last = lax.slice_in_dim(block, size - 1, None, axis=dim)
    first = lax.slice_in_dim(block, 0, 1, axis=dim)
    if count == 1:
        return last, first
    if count == 2:
        ends = block if size == 2 else jnp.concatenate([first, last], axis=dim)
        ends = lax.ppermute(ends, axis, [(0, 1), (1, 0)])
        return lax.slice_in_dim(ends, 1, 2, axis=dim), lax.slice_in_dim(ends, 0, 1, axis=dim)
    forward = [(i, (i + 1) % count) for i in range(count)]
    backward = [(target, source) for source, target in forward]
    return lax.ppermute(last, axis, forward), lax.ppermute(first, axis, backward)


def after(block, *others):
    return lax.optimization_barrier((block,) + others)[0]


def exchange(block, beside_x, beside_y):
    low, high = ends_of(block, "gx", 0)
    wide = jnp.concatenate([low, block, high], axis=0)
    first = beside_x()
    low, high = ends_of(after(wide, *first), "gy", 1)
    layers = jnp.concatenate([low, wide, high], axis=1)
    second = beside_y()
    low, high = ends_of(after(layers, *second), "gz", 2)
    return flat(layers), jnp.concatenate([flat(low), flat(high)], axis=0)


def column_constant(values, rows):
    ids = lax.broadcasted_iota(jnp.int32, (rows, 128), 0)
    out = jnp.zeros((rows, 128), jnp.float32)
    for row, value in enumerate(values):
        if value != 0.0:
            out = jnp.where(ids == row, jnp.float32(value), out)
    return out


def pair_inside(own, row):
    dx = own[0] - row(0)
    dy = own[1] - row(1)
    dz = own[2] - row(2)
    square = dx * dx + dy * dy + dz * dz
    radius = square * lax.rsqrt(jnp.maximum(square, TINY))
    return dx, dy, dz, jnp.maximum(1.0 - radius, 0.0)


def volume_pair(own, row):
    _, _, _, inside = pair_inside(own, row)
    second = inside * inside
    return ((second * second) * (1.25 - inside),)


def density_pair(own, row):
    dx, dy, dz, inside = pair_inside(own, row)
    third = inside * inside * inside
    value = third * (inside * (1.25 - inside))
    relative = (row(4) - own[4]) * dx + (row(5) - own[5]) * dy + (row(6) - own[6]) * dz
    volume = row(7)
    return (
        row(3) * value,
        volume * value,
        (volume * third) * relative,
    )


def force_pair(own, row):
    dx, dy, dz, inside = pair_inside(own, row)
    scaled = row(3) * (inside * inside * inside)
    relative = (own[4] - row(4)) * dx + (own[5] - row(5)) * dy + (own[6] - row(6)) * dz
    half = (own[10] + row(10)) / (own[8] + row(8))
    heat = own[9] + half
    push = (heat + (row(9) + half)) * scaled
    return (
        push * dx,
        push * dy,
        push * dz,
        (heat * scaled) * relative,
    )


def prepare_kernel(counts_hbm, offsets_hbm, velocity_hbm, mass_hbm, out_ref, *scratch):
    sources = (counts_hbm, offsets_hbm, velocity_hbm, mass_hbm)
    holds, sems = scratch[:4], scratch[4]
    copies = [
        pltpu.make_async_copy(source, hold, sems.at[i])
        for i, (source, hold) in enumerate(zip(sources, holds))
    ]
    for copy in copies:
        copy.start()
    for copy in copies:
        copy.wait()
    counts_ref, offsets_ref, velocity_ref, mass_ref = holds
    nx, ny, nz = mass_ref.shape[:3]
    for leaf, (x, y, z) in enumerate(itertools.product(range(nx), range(ny), range(nz))):
        for c in range(3):
            out_ref[leaf, c : c + 1, :] = offsets_ref[x, y, c, z : z + 1, :]
            out_ref[leaf, 4 + c : 5 + c, :] = velocity_ref[x, y, c, z : z + 1, :]
        out_ref[leaf, 3:4, :] = mass_ref[x, y, z : z + 1, :]
        number = counts_ref[x, y : y + 1, z : z + 1].astype(jnp.float32)
        out_ref[leaf, 7:8, :] = jnp.broadcast_to(number, (1, mass_ref.shape[3]))


def partners(grid):
    nx, ny, nz = grid
    parts = ([], [], [])
    for x, y, z in itertools.product(range(nx), range(ny), range(nz)):
        for part in parts:
            part.append([])
        for k, (ox, oy, oz) in enumerate(OFFSETS):
            tx, ty, tz = x + ox, y + oy, z + oz
            plane = (tx + 1) * (ny + 2) + ty + 1
            if not 0 <= tz < nz:
                parts[2][-1].append((k, plane + (0 if tz < 0 else (nx + 2) * (ny + 2))))
            elif 0 <= tx < nx and 0 <= ty < ny:
                parts[0][-1].append((k, (tx * ny + ty) * nz + tz))
            else:
                parts[1][-1].append((k, plane * nz + tz))
    return parts


def longest(part):
    return max(len(leaf) for leaf in part)


def list_tiles(part):
    return longest(part) + 1 + AHEAD


def split_place(start):
    return start & 127, lax.shift_right_logical(start, 7)


def put(list_ref, leaf, shift, tile, block, lanes):
    rolled = pltpu.roll(block, shift, axis=1)
    pltpu.store(list_ref.at[leaf, tile], rolled, mask=lanes >= shift)
    list_ref[leaf, tile + 1] = rolled


def close(list_ref, leaf, shift, tile, tail, lanes):
    pltpu.store(list_ref.at[leaf, tile], tail, mask=lanes >= shift)
    for step in range(1, AHEAD):
        list_ref[leaf, tile + step] = tail


def lane_ids(rows):
    return lax.broadcasted_iota(jnp.int32, (rows, 128), 1)


def pack_places(part, source_ref, list_ref, size_of, note):
    lanes = lane_ids(8)
    far = column_constant((FAR, FAR, FAR), 8)
    moves = [column_constant(offset, 8) for offset in OFFSETS]
    for leaf, found in enumerate(part):
        start = jnp.int32(0)
        for index, (k, place) in enumerate(found):
            shift, tile = split_place(start)
            note(leaf, index, shift, tile)
            put(list_ref, leaf, shift, tile, source_ref[place] + moves[k], lanes)
            start = start + size_of(leaf, k, place)
        shift, tile = split_place(start)
        note(leaf, len(found), shift, tile)
        note(leaf, None, shift, tile)
        close(list_ref, leaf, shift, tile, far, lanes)


def pack_side(part, source_ref, side_ref, shift_ref, tile_ref, tail):
    height = source_ref.shape[1]
    lanes = lane_ids(height)
    last = column_constant(tail, height)
    stride = longest(part) + 1
    for leaf, found in enumerate(part):
        for index, (_, place) in enumerate(found):
            at = leaf * stride + index
            put(side_ref, leaf, shift_ref[at], tile_ref[at], source_ref[place], lanes)
        at = leaf * stride + len(found)
        close(side_ref, leaf, shift_ref[at], tile_ref[at], last, lanes)


def widen_kernel(rows, block_ref, out_ref):
    for leaf in range(block_ref.shape[0]):
        for index, c in enumerate(rows):
            row = block_ref[leaf, c : c + 1, :]
            out_ref[leaf, index] = jnp.transpose(jnp.broadcast_to(row, (128, 128)))


def arrange_kernel(parts, *refs):
    mask_ref, refs = refs[0], refs[1:]
    count = len(parts)
    for i, part in enumerate(parts):
        counts_ref, source_ref = refs[i], refs[count + i]
        list_ref, shift_ref, tile_ref, last_ref = refs[2 * count + 4 * i : 2 * count + 4 * i + 4]
        stride = longest(part) + 1

        def size_of(leaf, k, place):
            return counts_ref[place] * mask_ref[leaf * 27 + k]

        def note(leaf, index, shift, tile):
            if index is None:
                last_ref[leaf] = tile
            else:
                shift_ref[leaf * stride + index] = shift
                tile_ref[leaf * stride + index] = tile

        pack_places(part, source_ref, list_ref, size_of, note)


def run_pairs(grid, pair, n_sums, count_of, last_of, own_of, row_of, before_ref, acc_ref):
    zero = jnp.zeros((8, 128), jnp.float32)

    def leaf_step(leaf, carry):
        count = count_of(leaf)
        steps = lax.shift_right_logical(last_of(leaf) + AHEAD, AHEAD.bit_length() - 1)

        def group_step(group, carry):
            places = [
                pl.ds(pl.multiple_of(group * (8 * GROUP) + 8 * part, 8), 8) for part in range(GROUP)
            ]
            owns = [own_of(leaf, at) for at in places]

            def partner_step(step, sums):
                for more in range(AHEAD):
                    rows = {}
                    at = step * AHEAD + more

                    def row(c):
                        if c not in rows:
                            rows[c] = jnp.broadcast_to(row_of(leaf, at, c), (8, 128))
                        return rows[c]

                    terms = [pair(own, row) for own in owns]
                    sums = tuple(
                        tuple(a + b for a, b in zip(old, new)) for old, new in zip(sums, terms)
                    )
                return sums

            start = tuple(
                tuple(zero if before_ref is None else before_ref[leaf, i, at, :] for i in range(n_sums))
                for at in places
            )
            sums = lax.fori_loop(0, steps, partner_step, start)
            for part, at in enumerate(places):
                for index in range(n_sums):
                    acc_ref[leaf, index, at, :] = sums[part][index]
            return carry

        groups = lax.shift_right_logical(count + (8 * GROUP - 1), (8 * GROUP).bit_length() - 1)
        return lax.fori_loop(0, groups, group_step, carry)

    lax.fori_loop(0, grid[0] * grid[1] * grid[2], leaf_step, 0)


def leaf_totals(grid, acc_ref, counts_ref):
    for leaf, index in enumerate(itertools.product(*map(range, grid))):
        sums = [
            jnp.sum(jnp.transpose(acc_ref[leaf, i]), axis=0, keepdims=True)
            for i in range(acc_ref.shape[1])
        ]
        yield index, leaf, sums, lax.broadcasted_iota(jnp.int32, (1, 128), 1) < counts_ref[leaf]


def own_reader(*pieces):
    def own_of(leaf, at):
        return {c: ref[leaf, i, at, :] for ref, channels in pieces for i, c in enumerate(channels)}

    return own_of


def row_reader(list_ref, side_ref=None, base=8):
    def row_of(leaf, at, c):
        if c < base:
            return list_ref[leaf, at, c : c + 1, :]
        return side_ref[leaf, at, c - base : c - base + 1, :]

    return row_of


def volume_kernel(grid, part, stage, *refs):
    refs = list(refs)
    out_ref, counts_ref, list_ref, last_ref = refs[-4:] if stage < 2 else refs[-5:-1]
    acc_ref = out_ref if stage < 2 else refs[-1]
    centers_ref = refs.pop(0) if stage else counts_ref
    source_ref, wide_ref = refs[:2]
    for place in range(source_ref.shape[0]):
        counts_ref[place] = source_ref[place, 7:8, :].astype(jnp.int32)[0, 0]

    def note(leaf, index, shift, tile):
        if index is None:
            last_ref[leaf] = tile

    pack_places(part, source_ref, list_ref, lambda leaf, k, place: counts_ref[place], note)
    run_pairs(
        grid, volume_pair, 1, lambda leaf: centers_ref[leaf], lambda leaf: last_ref[leaf],
        own_reader((wide_ref, WIDE)), row_reader(list_ref), refs[2] if stage else None, acc_ref,
    )
    if stage == 2:
        for index, leaf, sums, valid in leaf_totals(grid, acc_ref, centers_ref):
            out_ref[leaf] = jnp.where(valid, 1.0 / (1.0 + 4.0 * sums[0]), 1.0)


def density_kernel(grid, part, stage, *refs):
    counts_ref, shift_ref, tile_ref, last_ref, list_ref, wide_ref, source_ref = refs[:7]
    out_ref, side_ref = refs[-2:] if stage < 2 else refs[-3:-1]
    acc_ref = out_ref if stage < 2 else refs[-1]
    pack_side(part, source_ref, side_ref, shift_ref, tile_ref, ())
    run_pairs(
        grid, density_pair, 3, lambda leaf: counts_ref[leaf], lambda leaf: last_ref[leaf],
        own_reader((wide_ref, WIDE)), row_reader(list_ref, side_ref, 7), refs[7] if stage else None, acc_ref,
    )
    if stage == 2:
        own_ref, volume_ref, energy_ref = refs[8:11]
        for (x, y, z), leaf, sums, valid in leaf_totals(grid, acc_ref, counts_ref):
            density = (own_ref[leaf, 3:4, :] + 4.0 * sums[0]) / (volume_ref[leaf] + 4.0 * sums[1])
            density = jnp.where(valid, density, 1.0)
            energy = energy_ref[x, y, z : z + 1, :]
            out_ref[leaf, 0:1, :] = density
            out_ref[leaf, 1:2, :] = jnp.where(valid, (2.0 / 3.0) * energy / density, 0.0)
            out_ref[leaf, 2:3, :] = jnp.where(valid, jnp.maximum(20.0 * sums[2], 0.0), 0.0)
            out_ref[leaf, 3:4, :] = jnp.zeros_like(density)


def force_kernel(grid, part, stage, *refs):
    counts_ref, shift_ref, tile_ref, last_ref, list_ref, wide_ref, state_ref, source_ref = refs[:8]
    side_ref = refs[-1] if stage < 2 else refs[-2]
    acc_ref = refs[-2] if stage < 2 else refs[-1]
    pack_side(part, source_ref, side_ref, shift_ref, tile_ref, (1.0,))
    run_pairs(
        grid, force_pair, 4, lambda leaf: counts_ref[leaf], lambda leaf: last_ref[leaf],
        own_reader((wide_ref, WIDE), (state_ref, (8, 9, 10))), row_reader(list_ref, side_ref),
        refs[8] if stage else None, acc_ref,
    )
    if stage == 2:
        push_ref, heat_ref = refs[9:11]
        for (x, y, z), leaf, sums, valid in leaf_totals(grid, acc_ref, counts_ref):
            for c in range(3):
                push_ref[x, y, c, z : z + 1, :] = jnp.where(valid, 20.0 * sums[c], 0.0)
            heat_ref[x, y, z : z + 1, :] = jnp.where(valid, -20.0 * sums[3], 0.0)


def call(name, body, inputs, outs, scratch=(), cycles=0):
    def spec(x):
        scalar = x.dtype == jnp.int32 and len(x.shape) == 1
        return pl.BlockSpec(memory_space=pltpu.SMEM if scalar else pltpu.VMEM)

    return pl.pallas_call(
        body,
        out_shape=outs,
        in_specs=[spec(x) for x in inputs],
        out_specs=[spec(x) for x in outs],
        scratch_shapes=scratch,
        compiler_params=pltpu.CompilerParams(vmem_limit_bytes=ROOM),
        cost_estimate=pl.CostEstimate(flops=cycles * 4096, bytes_accessed=1 << 20, transcendentals=0),
        name=name,
    )(*inputs)


def floats(*shape):
    return jax.ShapeDtypeStruct(shape, jnp.float32)


def integers(*shape):
    return jax.ShapeDtypeStruct(shape, jnp.int32)


def flat(block):
    return block.reshape((-1,) + block.shape[3:])


def shards(offsets, velocity, mass, energy, partner_mask, counts):
    grid = counts.shape
    slots = offsets.shape[4]
    assert slots == 128
    leaves = grid[0] * grid[1] * grid[2]
    parts = partners(grid)
    inputs = (counts, jnp.swapaxes(offsets, 2, 3), jnp.swapaxes(velocity, 2, 3), mass)
    own = pl.pallas_call(
        prepare_kernel,
        out_shape=floats(leaves, 8, slots),
        in_specs=[pl.BlockSpec(memory_space=pltpu.HBM)] * 4,
        out_specs=pl.BlockSpec(memory_space=pltpu.VMEM),
        scratch_shapes=[pltpu.VMEM(x.shape, x.dtype) for x in inputs] + [pltpu.SemaphoreType.DMA((4,))],
        compiler_params=pltpu.CompilerParams(vmem_limit_bytes=ROOM),
        name="prepare",
    )(*inputs)
    mask = partner_mask.reshape(-1)
    wide = call(
        "widen", functools.partial(widen_kernel, WIDE), [own],
        [floats(leaves, len(WIDE), slots, slots)], cycles=2000,
    )[0]

    def packed_space(p, height):
        return pltpu.VMEM((leaves, list_tiles(parts[p]), height, slots), jnp.float32)

    def spread_sums(p, n_sums):
        shape = (leaves, n_sums, slots, slots)
        return ([floats(*shape)], []) if p < 2 else ([], [pltpu.VMEM(shape, jnp.float32)])

    def volume_part(p, source, centers=(), before=()):
        outs, own_space = spread_sums(p, 1)
        return call(
            f"volume_{p}", functools.partial(volume_kernel, grid, parts[p], p),
            [*centers, source, wide, *before],
            (outs or [floats(leaves, 1, slots)]) + [integers(source.shape[0])],
            [packed_space(p, 8), pltpu.SMEM((leaves,), jnp.int32)] + own_space, cycles=3000,
        )

    near_counts, lists, early = [], [], []

    def volume_own():
        part, number = volume_part(0, own)
        near_counts.append(number)
        early.append(part)
        return (part,)

    layers, ends = exchange(own.reshape(grid + (8, slots)), lambda: (wide,), volume_own)
    part, number = volume_part(1, layers, near_counts, early)
    volume, last_number = volume_part(2, ends, near_counts, [part])
    near_counts += [number, last_number]

    def arrange():
        outs = []
        for part in parts:
            stride = longest(part) + 1
            outs += [
                floats(leaves, list_tiles(part), 8, slots),
                integers(leaves * stride), integers(leaves * stride), integers(leaves),
            ]
        done = call(
            "arrange", functools.partial(arrange_kernel, parts), [mask, *near_counts, own, layers, ends],
            outs, cycles=2000,
        )
        lists.extend(tuple(done[4 * p : 4 * p + 4]) for p in range(3))
        return tuple(entry[0] for entry in lists)

    def density_part(p, source, more=()):
        packed, shifts, starts, last = lists[p]
        outs, own_space = spread_sums(p, 3)
        return call(
            f"density_{p}", functools.partial(density_kernel, grid, parts[p], p),
            [near_counts[0], shifts, starts, last, packed, wide, source, *more],
            outs or [floats(leaves, 4, slots)], [packed_space(p, 1)] + own_space, cycles=4000,
        )[0]

    def density_own():
        early[:] = [density_part(0, volume)]
        return tuple(early)

    volume_layers, volume_ends = exchange(volume.reshape(grid + (1, slots)), arrange, density_own)
    part = density_part(1, volume_layers, early)
    state = density_part(2, volume_ends, [part, own, volume, energy])

    wide_state = call(
        "widen_state", functools.partial(widen_kernel, (0, 1, 2)), [state],
        [floats(leaves, 3, slots, slots)], cycles=1000,
    )[0]

    def force_part(p, source, more=()):
        packed, shifts, starts, last = lists[p]
        outs, own_space = spread_sums(p, 4)
        return call(
            f"force_{p}", functools.partial(force_kernel, grid, parts[p], p),
            [near_counts[0], shifts, starts, last, packed, wide, wide_state, source, *more],
            outs or [floats(*grid[:2], 3, grid[2], slots), floats(*grid, slots)],
            [packed_space(p, 4)] + own_space, cycles=5000,
        )

    def force_own():
        early[:] = force_part(0, state)
        return tuple(early)

    state_layers, state_ends = exchange(state.reshape(grid + (4, slots)), lambda: (wide_state,), force_own)
    push, heat = force_part(2, state_ends, force_part(1, state_layers, early))
    return jnp.swapaxes(push, 2, 3), heat


def solution(mesh):
    placed = (
        P("gx", "gy", "gz", None, None),
        P("gx", "gy", "gz", None, None),
        P("gx", "gy", "gz", None),
        P("gx", "gy", "gz", None),
        P("gx", "gy", "gz", None),
        P("gx", "gy", "gz"),
    )
    return jax.shard_map(
        shards,
        mesh=mesh,
        in_specs=placed,
        out_specs=(P("gx", "gy", "gz", None, None), P("gx", "gy", "gz", None)),
        check_vma=False,
    )
```

```python
import functools
import itertools

import jax
import jax.numpy as jnp
from jax import lax
from jax.experimental import pallas as pl
from jax.experimental.pallas import tpu as pltpu
from jax.sharding import PartitionSpec as P

AXES = (("gx", 0), ("gy", 1), ("gz", 2))
FAR = 1024.0
TINY = 1e-30
ROOM = 6 << 20
GROUP = 4
WIDE = (0, 1, 2, 4, 5, 6)
OFFSETS = tuple(itertools.product((-1, 0, 1), repeat=3))


def ends_of(block, axis, dim):
    count = lax.axis_size(axis)
    size = block.shape[dim]
    last = lax.slice_in_dim(block, size - 1, None, axis=dim)
    first = lax.slice_in_dim(block, 0, 1, axis=dim)
    if count == 1:
        return last, first
    if count == 2:
        ends = block if size == 2 else jnp.concatenate([first, last], axis=dim)
        ends = lax.ppermute(ends, axis, [(0, 1), (1, 0)])
        return lax.slice_in_dim(ends, 1, 2, axis=dim), lax.slice_in_dim(ends, 0, 1, axis=dim)
    if count % 2:
        forward = [(i, (i + 1) % count) for i in range(count)]
        backward = [(target, source) for source, target in forward]
        return lax.ppermute(last, axis, forward), lax.ppermute(first, axis, backward)
    even = lax.axis_index(axis) % 2 == 0
    near_pairs = [(i, i + 1 - 2 * (i % 2)) for i in range(count)]
    far_pairs = [(i, (i - 1 + 2 * (i % 2)) % count) for i in range(count)]
    one = lax.ppermute(jnp.where(even, last, first), axis, near_pairs)
    two = lax.ppermute(jnp.where(even, first, last), axis, far_pairs)
    return jnp.where(even, two, one), jnp.where(even, one, two)


def after(block, *others):
    return lax.optimization_barrier((block,) + others)[0]


def exchange(block, beside_x, beside_y):
    low, high = ends_of(block, "gx", 0)
    wide = jnp.concatenate([low, block, high], axis=0)
    first = beside_x()
    low, high = ends_of(after(wide, *first), "gy", 1)
    layers = jnp.concatenate([low, wide, high], axis=1)
    second = beside_y()
    low, high = ends_of(after(layers, *second), "gz", 2)
    return flat(layers), jnp.concatenate([flat(low), flat(high)], axis=0)


def column_constant(values, rows):
    ids = lax.broadcasted_iota(jnp.int32, (rows, 128), 0)
    out = jnp.zeros((rows, 128), jnp.float32)
    for row, value in enumerate(values):
        if value != 0.0:
            out = jnp.where(ids == row, jnp.float32(value), out)
    return out


def pair_inside(own, row):
    dx = own[0] - row(0)
    dy = own[1] - row(1)
    dz = own[2] - row(2)
    square = dx * dx + dy * dy + dz * dz
    radius = square * lax.rsqrt(jnp.maximum(square, TINY))
    return dx, dy, dz, jnp.maximum(1.0 - radius, 0.0)


def volume_pair(own, row):
    _, _, _, inside = pair_inside(own, row)
    second = inside * inside
    return ((second * second) * (1.25 - inside),)


def density_pair(own, row):
    dx, dy, dz, inside = pair_inside(own, row)
    third = inside * inside * inside
    value = third * (inside * (1.25 - inside))
    relative = (row(4) - own[4]) * dx + (row(5) - own[5]) * dy + (row(6) - own[6]) * dz
    volume = row(7)
    return (
        row(3) * value,
        volume * value,
        (volume * third) * relative,
    )


def force_pair(own, row):
    dx, dy, dz, inside = pair_inside(own, row)
    scaled = row(3) * (inside * inside * inside)
    relative = (own[4] - row(4)) * dx + (own[5] - row(5)) * dy + (own[6] - row(6)) * dz
    half = (own[10] + row(10)) / (own[8] + row(8))
    heat = own[9] + half
    push = (heat + (row(9) + half)) * scaled
    return (
        push * dx,
        push * dy,
        push * dz,
        (heat * scaled) * relative,
    )


def prepare_kernel(counts_ref, base_ref, out_ref):
    nx, ny, channels, nz, slots = base_ref.shape
    for leaf, (x, y, z) in enumerate(itertools.product(range(nx), range(ny), range(nz))):
        for c in range(channels):
            out_ref[leaf, c : c + 1, :] = base_ref[x, y, c, z : z + 1, :]
        number = counts_ref[x, y : y + 1, z : z + 1].astype(jnp.float32)
        out_ref[leaf, channels : channels + 1, :] = jnp.broadcast_to(number, (1, slots))


def partners(grid):
    nx, ny, nz = grid
    parts = ([], [], [])
    for x, y, z in itertools.product(range(nx), range(ny), range(nz)):
        for part in parts:
            part.append([])
        for k, (ox, oy, oz) in enumerate(OFFSETS):
            tx, ty, tz = x + ox, y + oy, z + oz
            plane = (tx + 1) * (ny + 2) + ty + 1
            if not 0 <= tz < nz:
                parts[2][-1].append((k, plane + (0 if tz < 0 else (nx + 2) * (ny + 2))))
            elif 0 <= tx < nx and 0 <= ty < ny:
                parts[0][-1].append((k, (tx * ny + ty) * nz + tz))
            else:
                parts[1][-1].append((k, plane * nz + tz))
    return parts


def longest(part):
    return max(len(leaf) for leaf in part)


def list_tiles(part):
    return longest(part) + 2


def split_place(start):
    return start & 127, lax.shift_right_logical(start, 7)


def put(list_ref, leaf, shift, tile, block, lanes):
    rolled = pltpu.roll(block, shift, axis=1)
    pltpu.store(list_ref.at[leaf, tile], rolled, mask=lanes >= shift)
    list_ref[leaf, tile + 1] = rolled


def close(list_ref, leaf, shift, tile, tail, lanes):
    pltpu.store(list_ref.at[leaf, tile], tail, mask=lanes >= shift)


def lane_ids(rows):
    return lax.broadcasted_iota(jnp.int32, (rows, 128), 1)


def pack_places(part, source_ref, list_ref, size_of, note):
    lanes = lane_ids(8)
    far = column_constant((FAR, FAR, FAR), 8)
    moves = [column_constant(offset, 8) for offset in OFFSETS]
    for leaf, found in enumerate(part):
        start = jnp.int32(0)
        for index, (k, place) in enumerate(found):
            shift, tile = split_place(start)
            note(leaf, index, shift, tile)
            put(list_ref, leaf, shift, tile, source_ref[place] + moves[k], lanes)
            start = start + size_of(leaf, k, place)
        shift, tile = split_place(start)
        note(leaf, len(found), shift, tile)
        note(leaf, None, None, split_place(start + 127)[1])
        close(list_ref, leaf, shift, tile, far, lanes)


def pack_side(part, span, source_ref, side_ref, shift_ref, tile_ref, tail):
    height = source_ref.shape[1]
    lanes = lane_ids(height)
    last = column_constant(tail, height)
    stride = longest(part) + 1
    for leaf in range(*span):
        found = part[leaf]
        for index, (_, place) in enumerate(found):
            at = leaf * stride + index
            put(side_ref, leaf, shift_ref[at], tile_ref[at], source_ref[place], lanes)
        at = leaf * stride + len(found)
        close(side_ref, leaf, shift_ref[at], tile_ref[at], last, lanes)


def widen_kernel(rows, block_ref, out_ref):
    for leaf in range(block_ref.shape[0]):
        for index, c in enumerate(rows):
            row = block_ref[leaf, c : c + 1, :]
            out_ref[leaf, index] = jnp.transpose(jnp.broadcast_to(row, (128, 128)))


def read_counts(source_ref, counts_ref):
    for place in range(source_ref.shape[0]):
        counts_ref[place] = source_ref[place, 7:8, :].astype(jnp.int32)[0, 0]


def pack_masked(part, mask_ref, counts_ref, source_ref, list_ref, shift_ref, tile_ref, last_ref):
    stride = longest(part) + 1

    def size_of(leaf, k, place):
        return counts_ref[place] * mask_ref[leaf * 27 + k]

    def note(leaf, index, shift, tile):
        if index is None:
            last_ref[leaf] = tile
        else:
            shift_ref[leaf * stride + index] = shift
            tile_ref[leaf * stride + index] = tile

    pack_places(part, source_ref, list_ref, size_of, note)


def arrange_kernel(part, mask_ref, counts_ref, source_ref, *outs):
    pack_masked(part, mask_ref, counts_ref, source_ref, *outs)


def run_pairs(span, pair, n_sums, count_of, tiles_of, own_of, row_of, before_ref, acc_ref):
    zero = jnp.zeros((8, 128), jnp.float32)

    def leaf_step(leaf, carry):
        count = count_of(leaf)
        tiles = tiles_of(leaf)

        def group_step(group, carry):
            places = [
                pl.ds(pl.multiple_of(group * (8 * GROUP) + 8 * part, 8), 8) for part in range(GROUP)
            ]
            owns = [own_of(leaf, at) for at in places]

            def add_tile(tile, sums):
                rows = {}

                def row(c):
                    if c not in rows:
                        rows[c] = jnp.broadcast_to(row_of(leaf, tile, c), (8, 128))
                    return rows[c]

                terms = [pair(own, row) for own in owns]
                return tuple(tuple(a + b for a, b in zip(old, new)) for old, new in zip(sums, terms))

            def two_tiles(step, sums):
                return add_tile(2 * step + 1, add_tile(2 * step, sums))

            start = tuple(
                tuple(zero if before_ref is None else before_ref[leaf, i, at, :] for i in range(n_sums))
                for at in places
            )
            sums = lax.fori_loop(0, lax.shift_right_logical(tiles, 1), two_tiles, start)
            sums = lax.fori_loop(0, tiles & 1, lambda _, sums: add_tile(tiles - 1, sums), sums)
            for part, at in enumerate(places):
                for index in range(n_sums):
                    acc_ref[leaf, index, at, :] = sums[part][index]
            return carry

        groups = lax.shift_right_logical(count + (8 * GROUP - 1), (8 * GROUP).bit_length() - 1)
        return lax.fori_loop(0, groups, group_step, carry)

    lax.fori_loop(*span, leaf_step, 0)


def lane_sums(blocks):
    rows = []
    left = lane_ids(128) < 64
    for i in range(0, len(blocks) - 1, 2):
        one, two = blocks[i : i + 2]
        both = jnp.where(left, one, two) + pltpu.roll(jnp.where(left, two, one), 64, axis=1)
        both = jnp.transpose(both)
        rows += [jnp.sum(half, axis=0, keepdims=True) for half in (both[:64], both[64:])]
    if len(blocks) % 2:
        rows.append(jnp.sum(jnp.transpose(blocks[-1]), axis=0, keepdims=True))
    return rows


def leaf_totals(grid, acc_ref, counts_ref):
    for leaf, index in enumerate(itertools.product(*map(range, grid))):
        sums = lane_sums([acc_ref[leaf, i] for i in range(acc_ref.shape[1])])
        yield index, leaf, sums, lax.broadcasted_iota(jnp.int32, (1, 128), 1) < counts_ref[leaf]


def own_reader(*pieces):
    def own_of(leaf, at):
        return {c: ref[leaf, i, at, :] for ref, channels in pieces for i, c in enumerate(channels)}

    return own_of


def row_reader(list_ref, side_ref=None, base=8):
    def row_of(leaf, at, c):
        if c < base:
            return list_ref[leaf, at, c : c + 1, :]
        return side_ref[leaf, at, c - base : c - base + 1, :]

    return row_of


def volume_kernel(grid, part, stage, *refs):
    refs = list(refs)
    centers_ref = refs.pop(0) if stage else None
    mask_ref = refs.pop(0) if stage < 2 else None
    source_ref, wide_ref = refs[:2]
    before_ref = refs[2] if stage else None
    out_ref, counts_ref, *masked_refs = refs[3 if stage else 2 :]
    list_ref, last_ref = masked_refs[-2:] if stage < 2 else masked_refs[-3:-1]
    acc_ref = out_ref if stage < 2 else refs[-1]
    if centers_ref is None:
        centers_ref = counts_ref
    read_counts(source_ref, counts_ref)

    def note(leaf, index, shift, tile):
        if index is None:
            last_ref[leaf] = tile

    pack_places(part, source_ref, list_ref, lambda leaf, k, place: counts_ref[place], note)
    if stage < 2:
        pack_masked(part, mask_ref, counts_ref, source_ref, *masked_refs[:4])
    run_pairs(
        (0, len(part)), volume_pair, 1, lambda leaf: centers_ref[leaf], lambda leaf: last_ref[leaf],
        own_reader((wide_ref, WIDE)), row_reader(list_ref), before_ref, acc_ref,
    )
    if stage == 2:
        for index, leaf, sums, valid in leaf_totals(grid, acc_ref, centers_ref):
            out_ref[leaf] = jnp.where(valid, 1.0 / (1.0 + 4.0 * sums[0]), 1.0)


def density_kernel(grid, part, stage, span, *refs):
    counts_ref, shift_ref, tile_ref, last_ref, list_ref, wide_ref, source_ref = refs[:7]
    out_ref, side_ref = refs[-2:] if stage < 2 else refs[-3:-1]
    acc_ref = out_ref if stage < 2 else refs[-1]
    pack_side(part, span, source_ref, side_ref, shift_ref, tile_ref, ())
    run_pairs(
        span, density_pair, 3, lambda leaf: counts_ref[leaf], lambda leaf: last_ref[leaf],
        own_reader((wide_ref, WIDE)), row_reader(list_ref, side_ref, 7), refs[7] if stage else None, acc_ref,
    )
    if stage == 2:
        own_ref, volume_ref, energy_ref = refs[8:11]
        for (x, y, z), leaf, sums, valid in leaf_totals(grid, acc_ref, counts_ref):
            density = (own_ref[leaf, 3:4, :] + 4.0 * sums[0]) / (volume_ref[leaf] + 4.0 * sums[1])
            density = jnp.where(valid, density, 1.0)
            energy = energy_ref[x, y, z : z + 1, :]
            out_ref[leaf, 0:1, :] = density
            out_ref[leaf, 1:2, :] = jnp.where(valid, (2.0 / 3.0) * energy / density, 0.0)
            out_ref[leaf, 2:3, :] = jnp.where(valid, jnp.maximum(20.0 * sums[2], 0.0), 0.0)
            out_ref[leaf, 3:4, :] = jnp.zeros_like(density)


def force_kernel(grid, part, stage, span, *refs):
    counts_ref, shift_ref, tile_ref, last_ref, list_ref, wide_ref, state_ref, source_ref = refs[:8]
    side_ref = refs[-1] if stage < 2 else refs[-2]
    acc_ref = refs[-2] if stage < 2 else refs[-1]
    pack_side(part, span, source_ref, side_ref, shift_ref, tile_ref, (1.0,))
    run_pairs(
        span, force_pair, 4, lambda leaf: counts_ref[leaf], lambda leaf: last_ref[leaf],
        own_reader((wide_ref, WIDE), (state_ref, (8, 9, 10))), row_reader(list_ref, side_ref),
        refs[8] if stage else None, acc_ref,
    )
    if stage == 2:
        push_ref, heat_ref = refs[9:11]
        for (x, y, z), leaf, sums, valid in leaf_totals(grid, acc_ref, counts_ref):
            for c in range(3):
                push_ref[x, y, c, z : z + 1, :] = jnp.where(valid, 20.0 * sums[c], 0.0)
            heat_ref[x, y, z : z + 1, :] = jnp.where(valid, -20.0 * sums[3], 0.0)


def call(name, body, inputs, outs, scratch=(), cycles=0, aliases=()):
    def spec(x):
        scalar = x.dtype == jnp.int32 and len(x.shape) == 1
        return pl.BlockSpec(memory_space=pltpu.SMEM if scalar else pltpu.VMEM)

    return pl.pallas_call(
        body,
        out_shape=outs,
        in_specs=[spec(x) for x in inputs],
        out_specs=[spec(x) for x in outs],
        scratch_shapes=scratch,
        input_output_aliases=dict(aliases),
        compiler_params=pltpu.CompilerParams(vmem_limit_bytes=ROOM),
        cost_estimate=pl.CostEstimate(flops=cycles * 4096, bytes_accessed=1 << 20, transcendentals=0),
        name=name,
    )(*inputs)


def floats(*shape):
    return jax.ShapeDtypeStruct(shape, jnp.float32)


def integers(*shape):
    return jax.ShapeDtypeStruct(shape, jnp.int32)


def flat(block):
    return block.reshape((-1,) + block.shape[3:])


def shards(offsets, velocity, mass, energy, partner_mask, counts):
    grid = counts.shape
    slots = offsets.shape[4]
    assert slots == 128
    leaves = grid[0] * grid[1] * grid[2]
    parts = partners(grid)
    pieces = [jnp.swapaxes(x, 2, 3) for x in (offsets, mass[:, :, :, None], velocity)]
    base = jnp.concatenate(pieces, axis=2)
    own = call("prepare", prepare_kernel, [counts, base], [floats(leaves, 8, slots)])[0]
    mask = partner_mask.reshape(-1)
    wide = call(
        "widen", functools.partial(widen_kernel, WIDE), [own],
        [floats(leaves, len(WIDE), slots, slots)], cycles=2000,
    )[0]

    def packed_space(p, height):
        return pltpu.VMEM((leaves, list_tiles(parts[p]), height, slots), jnp.float32)

    def spread_sums(p, n_sums):
        shape = (leaves, n_sums, slots, slots)
        return ([floats(*shape)], []) if p < 2 else ([], [pltpu.VMEM(shape, jnp.float32)])

    def masked_list(p):
        part = parts[p]
        stride = longest(part) + 1
        return [
            floats(leaves, list_tiles(part), 8, slots),
            integers(leaves * stride), integers(leaves * stride), integers(leaves),
        ]

    near_counts, lists, early = [], [], []

    def volume_part(p, source, more=()):
        outs, own_space = spread_sums(p, 1)
        outs = (outs or [floats(leaves, 1, slots)]) + [integers(source.shape[0])]
        if p < 2:
            outs += masked_list(p)
        out, number, *packed = call(
            f"volume_{p}", functools.partial(volume_kernel, grid, parts[p], p),
            near_counts[:1] + ([mask] if p < 2 else []) + [source, wide, *more], outs,
            [packed_space(p, 8), pltpu.SMEM((leaves,), jnp.int32)] + own_space, cycles=3000,
        )
        near_counts.append(number)
        if packed:
            lists.append(packed)
        return out

    def volume_own():
        early.append(volume_part(0, own))
        return tuple(early)

    layers, ends = exchange(own.reshape(grid + (8, slots)), lambda: (wide,), volume_own)
    volume = volume_part(2, ends, [volume_part(1, layers, early)])

    def arrange():
        lists.append(
            call(
                "arrange", functools.partial(arrange_kernel, parts[2]), [mask, near_counts[2], ends],
                masked_list(2), cycles=1000,
            )
        )
        return (lists[2][0],)

    def density_part(p, source, more=(), span=(0, leaves)):
        packed, shifts, starts, last = lists[p]
        outs, own_space = spread_sums(p, 3)
        return call(
            f"density_{p}", functools.partial(density_kernel, grid, parts[p], p, span),
            [near_counts[0], shifts, starts, last, packed, wide, source, *more],
            outs or [floats(leaves, 4, slots)], [packed_space(p, 1)] + own_space, cycles=4000,
        )[0]

    def density_own():
        early[:] = [density_part(0, volume)]
        return tuple(early)

    volume_layers, volume_ends = exchange(volume.reshape(grid + (1, slots)), arrange, density_own)
    part = density_part(1, volume_layers, early)
    state = density_part(2, volume_ends, [part, own, volume, energy])

    wide_state = call(
        "widen_state", functools.partial(widen_kernel, (0, 1, 2)), [state],
        [floats(leaves, 3, slots, slots)], cycles=1000,
    )[0]

    def force_part(p, source, more=(), span=(0, leaves)):
        packed, shifts, starts, last = lists[p]
        outs, own_space = spread_sums(p, 4)
        return call(
            f"force_{p}", functools.partial(force_kernel, grid, parts[p], p, span),
            [near_counts[0], shifts, starts, last, packed, wide, wide_state, source, *more],
            outs or [floats(*grid[:2], 3, grid[2], slots), floats(*grid, slots)],
            [packed_space(p, 4)] + own_space, cycles=5000,
            aliases=[(8, 0)] if p == 0 and more else (),
        )

    def force_own(span):
        def run():
            early[:] = force_part(0, state, early if span[0] else (), span)
            return tuple(early)

        return run

    cut = 3 * leaves // 8
    state_layers, state_ends = exchange(
        state.reshape(grid + (4, slots)), force_own((0, cut)), force_own((cut, leaves))
    )
    push, heat = force_part(2, state_ends, force_part(1, state_layers, early))
    return jnp.swapaxes(push, 2, 3), heat


def solution(mesh):
    placed = (
        P("gx", "gy", "gz", None, None),
        P("gx", "gy", "gz", None, None),
        P("gx", "gy", "gz", None),
        P("gx", "gy", "gz", None),
        P("gx", "gy", "gz", None),
        P("gx", "gy", "gz"),
    )
    return jax.shard_map(
        shards,
        mesh=mesh,
        in_specs=placed,
        out_specs=(P("gx", "gy", "gz", None, None), P("gx", "gy", "gz", None)),
        check_vma=False,
    )
```

```python
import functools
import itertools

import jax
import jax.numpy as jnp
from jax import lax
from jax.experimental import pallas as pl
from jax.experimental.pallas import tpu as pltpu
from jax.sharding import PartitionSpec as P

AXES = (("gx", 0), ("gy", 1), ("gz", 2))
FAR = 1024.0
TINY = 1e-30
ROOM = 6 << 20
GROUP = 4
WIDE = (0, 1, 2, 4, 5, 6)
OFFSETS = tuple(itertools.product((-1, 0, 1), repeat=3))


def ends_of(block, axis, dim):
    count = lax.axis_size(axis)
    size = block.shape[dim]
    last = lax.slice_in_dim(block, size - 1, None, axis=dim)
    first = lax.slice_in_dim(block, 0, 1, axis=dim)
    if count == 1:
        return first, last, True
    if count == 2:
        ends = block if size == 2 else jnp.concatenate([first, last], axis=dim)
        ends = lax.ppermute(ends, axis, [(0, 1), (1, 0)])
        return lax.slice_in_dim(ends, 0, 1, axis=dim), lax.slice_in_dim(ends, 1, 2, axis=dim), True
    if count % 2:
        forward = [(i, (i + 1) % count) for i in range(count)]
        backward = [(target, source) for source, target in forward]
        return lax.ppermute(first, axis, backward), lax.ppermute(last, axis, forward), True
    even = lax.axis_index(axis) % 2 == 0
    near_pairs = [(i, i + 1 - 2 * (i % 2)) for i in range(count)]
    far_pairs = [(i, (i - 1 + 2 * (i % 2)) % count) for i in range(count)]
    one = lax.ppermute(jnp.where(even, last, first), axis, near_pairs)
    two = lax.ppermute(jnp.where(even, first, last), axis, far_pairs)
    return one, two, even


def low_and_high(block, axis, dim):
    one, two, one_is_high = ends_of(block, axis, dim)
    if one_is_high is True:
        return two, one
    return jnp.where(one_is_high, two, one), jnp.where(one_is_high, one, two)


def after(block, *others):
    return lax.optimization_barrier((block,) + others)[0]


def exchange(block, beside_x, beside_y):
    low, high = low_and_high(block, "gx", 0)
    wide = jnp.concatenate([low, block, high], axis=0)
    first = beside_x()
    low, high = low_and_high(after(wide, *first), "gy", 1)
    layers = jnp.concatenate([low, wide, high], axis=1)
    second = beside_y()
    one, two, one_is_high = ends_of(after(layers, *second), "gz", 2)
    return flat(layers), flat(one), flat(two), one_is_high


def column_constant(values, rows):
    ids = lax.broadcasted_iota(jnp.int32, (rows, 128), 0)
    out = jnp.zeros((rows, 128), jnp.float32)
    for row, value in enumerate(values):
        if value != 0.0:
            out = jnp.where(ids == row, jnp.float32(value), out)
    return out


def apart(own, row):
    return own[0] - row(0), own[1] - row(1), own[2] - row(2)


def volume_pair(own, row, keep):
    dx, dy, dz = apart(own, row)
    square = dx * dx + dy * dy + dz * dz
    radius = square * lax.rsqrt(jnp.maximum(square, TINY))
    inside = jnp.maximum(1.0 - radius, 0.0)
    keep[...] = inside
    second = inside * inside
    return ((second * second) * (1.25 - inside),)


def density_pair(own, row, kept):
    dx, dy, dz = apart(own, row)
    inside = kept[...]
    third = inside * inside * inside
    value = third * (inside * (1.25 - inside))
    relative = (row(4) - own[4]) * dx + (row(5) - own[5]) * dy + (row(6) - own[6]) * dz
    volume = row(7)
    return (
        row(3) * value,
        volume * value,
        (volume * third) * relative,
    )


def force_pair(own, row, kept):
    dx, dy, dz = apart(own, row)
    inside = kept[...]
    scaled = row(3) * (inside * inside * inside)
    relative = (own[4] - row(4)) * dx + (own[5] - row(5)) * dy + (own[6] - row(6)) * dz
    half = (own[10] + row(10)) / (own[8] + row(8))
    heat = own[9] + half
    push = (heat + (row(9) + half)) * scaled
    return (
        push * dx,
        push * dy,
        push * dz,
        (heat * scaled) * relative,
    )


def prepare_kernel(counts_ref, base_ref, out_ref):
    nx, ny, channels, nz, slots = base_ref.shape
    for leaf, (x, y, z) in enumerate(itertools.product(range(nx), range(ny), range(nz))):
        for c in range(channels):
            out_ref[leaf, c : c + 1, :] = base_ref[x, y, c, z : z + 1, :]
        number = counts_ref[x, y : y + 1, z : z + 1].astype(jnp.float32)
        out_ref[leaf, channels : channels + 1, :] = jnp.broadcast_to(number, (1, slots))


def partners(grid):
    nx, ny, nz = grid
    parts = ([], [])
    for x, y, z in itertools.product(range(nx), range(ny), range(nz)):
        for part in parts:
            part.append([])
        for k, (ox, oy, oz) in enumerate(OFFSETS):
            tx, ty, tz = x + ox, y + oy, z + oz
            if 0 <= tz < nz:
                if 0 <= tx < nx and 0 <= ty < ny:
                    parts[0][-1].append((k, (tx * ny + ty) * nz + tz))
                else:
                    parts[1][-1].append((k, ((tx + 1) * (ny + 2) + ty + 1) * nz + tz))
    return parts


class Layers:
    def __init__(self, grid, part):
        self.lists = part
        self.mask_count = 27 * len(part)

    def bind(self, flag):
        self.moves = [column_constant(offset, 8) for offset in OFFSETS]

    def leaf(self, index):
        return index

    def mask_at(self, index, k):
        return index * 27 + k

    def move(self, k):
        return self.moves[k]


class Side:
    def __init__(self, grid, when):
        nx, ny, nz = grid
        self.depth, self.when = nz, when
        self.mask_count = 27 * nx * ny * nz
        columns = [(k, OFFSETS[k][:2]) for k in range(1, 27, 3)]
        self.lists = [
            [(k, (x + ox + 1) * (ny + 2) + y + oy + 1) for k, (ox, oy) in columns]
            for x, y in itertools.product(range(nx), range(ny))
        ]

    def bind(self, flag):
        self.high = flag if self.when else 1 - flag
        heights = lax.broadcasted_iota(jnp.int32, (8, 128), 0)
        along = jnp.where(heights == 2, (2 * self.high - 1).astype(jnp.float32), 0.0)
        self.moves = {k: column_constant(OFFSETS[k][:2], 8) + along for k in range(1, 27, 3)}

    def leaf(self, index):
        return index * self.depth + self.high * (self.depth - 1)

    def mask_at(self, index, k):
        return self.leaf(index) * 27 + (2 * self.high - 1) + k

    def move(self, k):
        return self.moves[k]


def longest(lists):
    return max(len(found) for found in lists)


def list_tiles(lists):
    return longest(lists) + 2


def split_place(start):
    return start & 127, lax.shift_right_logical(start, 7)


def put(list_ref, leaf, shift, tile, block, lanes):
    rolled = pltpu.roll(block, shift, axis=1)
    pltpu.store(list_ref.at[leaf, tile], rolled, mask=lanes >= shift)
    list_ref[leaf, tile + 1] = rolled


def close(list_ref, leaf, shift, tile, tail, lanes):
    pltpu.store(list_ref.at[leaf, tile], tail, mask=lanes >= shift)


def lane_ids(rows):
    return lax.broadcasted_iota(jnp.int32, (rows, 128), 1)


def pack_places(part, mask_ref, counts_ref, source_ref, list_ref, shift_ref, tile_ref, last_ref, all_ref):
    lanes = lane_ids(8)
    only_places = lax.broadcasted_iota(jnp.int32, (8, 128), 0) < 3
    far = column_constant((FAR, FAR, FAR), 8)
    stride = longest(part.lists) + 1
    for index, found in enumerate(part.lists):
        start = jnp.int32(0)
        for number, (k, place) in enumerate(found):
            shift, tile = split_place(start)
            shift_ref[index * stride + number] = shift
            tile_ref[index * stride + number] = tile
            put(list_ref, index, shift, tile, source_ref[place] + part.move(k), lanes)
            start = start + counts_ref[place] * mask_ref[part.mask_at(index, k)]
        shift, tile = split_place(start)
        shift_ref[index * stride + len(found)] = shift
        tile_ref[index * stride + len(found)] = tile
        last_ref[index] = split_place(start + 127)[1]
        for k, place in found:
            shift, tile = split_place(start)
            block = jnp.where(only_places, source_ref[place] + part.move(k), 0.0)
            put(list_ref, index, shift, tile, block, lanes)
            start = start + counts_ref[place] * (1 - mask_ref[part.mask_at(index, k)])
        shift, tile = split_place(start)
        close(list_ref, index, shift, tile, far, lanes)
        all_ref[index] = split_place(start + 127)[1]


def pack_side(part, span, source_ref, side_ref, shift_ref, tile_ref, tail):
    height = source_ref.shape[1]
    lanes = lane_ids(height)
    last = column_constant(tail, height)
    stride = longest(part.lists) + 1
    for index in range(*span):
        found = part.lists[index]
        for number, (_, place) in enumerate(found):
            at = index * stride + number
            put(side_ref, index, shift_ref[at], tile_ref[at], source_ref[place], lanes)
        at = index * stride + len(found)
        close(side_ref, index, shift_ref[at], tile_ref[at], last, lanes)


def widen_kernel(rows, block_ref, out_ref):
    for leaf in range(block_ref.shape[0]):
        for index, c in enumerate(rows):
            row = block_ref[leaf, c : c + 1, :]
            out_ref[leaf, index] = jnp.transpose(jnp.broadcast_to(row, (128, 128)))


def read_counts(source_ref, counts_ref):
    for place in range(source_ref.shape[0]):
        counts_ref[place] = source_ref[place, 7:8, :].astype(jnp.int32)[0, 0]


def run_pairs(part, span, pair, n_sums, counts_ref, tiles_ref, own_of, row_of, kept_ref, before_ref, acc_ref):
    zero = jnp.zeros((8, 128), jnp.float32)

    def leaf_step(index, carry):
        leaf = part.leaf(index)
        count = counts_ref[leaf]
        tiles = tiles_ref[index]

        def group_step(group, carry):
            places = [
                pl.ds(pl.multiple_of(group * (8 * GROUP) + 8 * chunk, 8), 8) for chunk in range(GROUP)
            ]
            owns = [own_of(leaf, at) for at in places]

            def add_tile(tile, sums):
                rows = {}

                def row(c):
                    if c not in rows:
                        rows[c] = jnp.broadcast_to(row_of(index, tile, c), (8, 128))
                    return rows[c]

                terms = [
                    pair(own, row, kept_ref.at[index, tile, at, :]) for own, at in zip(owns, places)
                ]
                return tuple(tuple(a + b for a, b in zip(old, new)) for old, new in zip(sums, terms))

            def two_tiles(step, sums):
                return add_tile(2 * step + 1, add_tile(2 * step, sums))

            start = tuple(
                tuple(zero if before_ref is None else before_ref[leaf, i, at, :] for i in range(n_sums))
                for at in places
            )
            sums = lax.fori_loop(0, lax.shift_right_logical(tiles, 1), two_tiles, start)
            sums = lax.fori_loop(0, tiles & 1, lambda _, sums: add_tile(tiles - 1, sums), sums)
            for at, total in zip(places, sums):
                for i in range(n_sums):
                    acc_ref[leaf, i, at, :] = total[i]
            return carry

        groups = lax.shift_right_logical(count + (8 * GROUP - 1), (8 * GROUP).bit_length() - 1)
        return lax.fori_loop(0, groups, group_step, carry)

    lax.fori_loop(*span, leaf_step, 0)


def lane_sums(blocks):
    rows = []
    left = lane_ids(128) < 64
    for i in range(0, len(blocks) - 1, 2):
        one, two = blocks[i : i + 2]
        both = jnp.where(left, one, two) + pltpu.roll(jnp.where(left, two, one), 64, axis=1)
        both = jnp.transpose(both)
        rows += [jnp.sum(half, axis=0, keepdims=True) for half in (both[:64], both[64:])]
    if len(blocks) % 2:
        rows.append(jnp.sum(jnp.transpose(blocks[-1]), axis=0, keepdims=True))
    return rows


def leaf_totals(grid, acc_ref, counts_ref):
    for leaf, index in enumerate(itertools.product(*map(range, grid))):
        sums = lane_sums([acc_ref[leaf, i] for i in range(acc_ref.shape[1])])
        yield index, leaf, sums, lax.broadcasted_iota(jnp.int32, (1, 128), 1) < counts_ref[leaf]


def own_reader(*pieces):
    def own_of(leaf, at):
        return {c: ref[leaf, i, at, :] for ref, channels in pieces for i, c in enumerate(channels)}

    return own_of


def row_reader(list_ref, side_ref=None, base=8):
    def row_of(leaf, at, c):
        if c < base:
            return list_ref[leaf, at, c : c + 1, :]
        return side_ref[leaf, at, c - base : c - base + 1, :]

    return row_of


def volume_kernel(grid, part, stage, *refs):
    refs = list(refs)
    numbers_ref = refs.pop(0) if stage else None
    mask_ref, source_ref, wide_ref = refs[:3]
    before_ref = refs[3] if stage else None
    acc_ref, counts_ref, list_ref, shift_ref, tile_ref, last_ref, kept_ref = refs[4 if stage else 3 :][:7]
    all_ref = refs[-1]
    read_counts(source_ref, counts_ref)
    if numbers_ref is None:
        numbers_ref = counts_ref
        numbers_ref[source_ref.shape[0]] = mask_ref[part.mask_count]
    part.bind(mask_ref[part.mask_count])
    pack_places(part, mask_ref, counts_ref, source_ref, list_ref, shift_ref, tile_ref, last_ref, all_ref)
    run_pairs(
        part, (0, len(part.lists)), volume_pair, 1, numbers_ref, all_ref,
        own_reader((wide_ref, WIDE)), row_reader(list_ref), kept_ref, before_ref, acc_ref,
    )
    if stage == 3:
        out_ref = refs[-2]
        for index, leaf, sums, valid in leaf_totals(grid, acc_ref, numbers_ref):
            out_ref[leaf] = jnp.where(valid, 1.0 / (1.0 + 4.0 * sums[0]), 1.0)


def density_kernel(grid, part, stage, span, *refs):
    numbers_ref, list_ref, shift_ref, tile_ref, last_ref, kept_ref, wide_ref, source_ref = refs[:8]
    before_ref = refs[8] if stage or span[0] else None
    acc_ref = refs[12 if stage == 3 else 9 if before_ref is not None else 8]
    side_ref = refs[-1]
    part.bind(numbers_ref[numbers_ref.shape[0] - 1])
    pack_side(part, span, source_ref, side_ref, shift_ref, tile_ref, ())
    run_pairs(
        part, span, density_pair, 3, numbers_ref, last_ref, own_reader((wide_ref, WIDE)),
        row_reader(list_ref, side_ref, 7), kept_ref, before_ref if stage else None, acc_ref,
    )
    if stage == 3:
        own_ref, volume_ref, energy_ref = refs[9:12]
        out_ref = refs[13]
        for (x, y, z), leaf, sums, valid in leaf_totals(grid, acc_ref, numbers_ref):
            density = (own_ref[leaf, 3:4, :] + 4.0 * sums[0]) / (volume_ref[leaf] + 4.0 * sums[1])
            density = jnp.where(valid, density, 1.0)
            energy = energy_ref[x, y, z : z + 1, :]
            out_ref[leaf, 0:1, :] = density
            out_ref[leaf, 1:2, :] = jnp.where(valid, (2.0 / 3.0) * energy / density, 0.0)
            out_ref[leaf, 2:3, :] = jnp.where(valid, jnp.maximum(20.0 * sums[2], 0.0), 0.0)
            out_ref[leaf, 3:4, :] = jnp.zeros_like(density)


def force_kernel(grid, part, stage, span, *refs):
    numbers_ref, list_ref, shift_ref, tile_ref, last_ref, kept_ref, wide_ref, state_ref, source_ref = refs[:9]
    before_ref = refs[9] if stage or span[0] else None
    acc_ref = refs[10 if before_ref is not None else 9]
    side_ref = refs[-1]
    part.bind(numbers_ref[numbers_ref.shape[0] - 1])
    pack_side(part, span, source_ref, side_ref, shift_ref, tile_ref, (1.0,))
    run_pairs(
        part, span, force_pair, 4, numbers_ref, last_ref,
        own_reader((wide_ref, WIDE), (state_ref, (8, 9, 10))), row_reader(list_ref, side_ref),
        kept_ref, before_ref if stage else None, acc_ref,
    )
    if stage == 3:
        push_ref, heat_ref = refs[11:13]
        for (x, y, z), leaf, sums, valid in leaf_totals(grid, acc_ref, numbers_ref):
            for c in range(3):
                push_ref[x, y, c, z : z + 1, :] = jnp.where(valid, 20.0 * sums[c], 0.0)
            heat_ref[x, y, z : z + 1, :] = jnp.where(valid, -20.0 * sums[3], 0.0)


def call(name, body, inputs, outs, scratch=(), cycles=0, aliases=()):
    def spec(x):
        scalar = x.dtype == jnp.int32 and len(x.shape) == 1
        return pl.BlockSpec(memory_space=pltpu.SMEM if scalar else pltpu.VMEM)

    return pl.pallas_call(
        body,
        out_shape=outs,
        in_specs=[spec(x) for x in inputs],
        out_specs=[spec(x) for x in outs],
        scratch_shapes=scratch,
        input_output_aliases=dict(aliases),
        compiler_params=pltpu.CompilerParams(vmem_limit_bytes=ROOM),
        cost_estimate=pl.CostEstimate(flops=cycles * 4096, bytes_accessed=1 << 20, transcendentals=0),
        name=name,
    )(*inputs)


def floats(*shape):
    return jax.ShapeDtypeStruct(shape, jnp.float32)


def integers(*shape):
    return jax.ShapeDtypeStruct(shape, jnp.int32)


def flat(block):
    return block.reshape((-1,) + block.shape[3:])


def shards(offsets, velocity, mass, energy, partner_mask, counts):
    grid = counts.shape
    slots = offsets.shape[4]
    assert slots == 128
    leaves = grid[0] * grid[1] * grid[2]
    parts = [Layers(grid, part) for part in partners(grid)] + [Side(grid, True), Side(grid, False)]
    pieces = [jnp.swapaxes(x, 2, 3) for x in (offsets, mass[:, :, :, None], velocity)]
    base = jnp.concatenate(pieces, axis=2)
    own = call("prepare", prepare_kernel, [counts, base], [floats(leaves, 8, slots)])[0]
    one_is_high = jnp.ones((1,), jnp.int32)
    if lax.axis_size("gz") > 2 and lax.axis_size("gz") % 2 == 0:
        one_is_high = 1 - lax.axis_index("gz").astype(jnp.int32)[None] % 2
    mask = jnp.concatenate([partner_mask.reshape(-1), one_is_high])
    wide = call(
        "widen", functools.partial(widen_kernel, WIDE), [own],
        [floats(leaves, len(WIDE), slots, slots)], cycles=2000,
    )[0]

    cut = 3 * leaves // 8

    def side_space(p, height):
        lists = parts[p].lists
        return pltpu.VMEM((len(lists), list_tiles(lists), height, slots), jnp.float32)

    def spread(n_sums):
        return floats(leaves, n_sums, slots, slots)

    def list_outs(p):
        lists = parts[p].lists
        count, tiles = len(lists), list_tiles(lists)
        numbers = integers(count * (longest(lists) + 1))
        return [
            floats(count, tiles, 8, slots), numbers, numbers, integers(count),
            floats(count, tiles, slots, slots),
        ]

    numbers, packs = [], []

    def volume_part(p, source, before=()):
        inputs = numbers[:1] + [mask, source, wide, *before]
        outs = [spread(1), integers(source.shape[0] + (p == 0))] + list_outs(p)
        acc, number, *packed = call(
            f"volume_{p}", functools.partial(volume_kernel, grid, parts[p], p), inputs,
            outs + ([floats(leaves, 1, slots)] if p == 3 else []),
            [pltpu.SMEM((len(parts[p].lists),), jnp.int32)], cycles=3000,
            aliases=[(len(inputs) - 1, 0)] if before else (),
        )
        numbers.append(number)
        packs.append(packed[:5])
        return [packed[5] if p == 3 else acc]

    def density_part(p, source, before=(), more=(), span=None):
        span = span or (0, len(parts[p].lists))
        return call(
            f"density_{p}", functools.partial(density_kernel, grid, parts[p], p, span),
            [numbers[0], *packs[p], wide, source, *before, *more],
            [spread(3)] + ([floats(leaves, 4, slots)] if p == 3 else []),
            [side_space(p, 1)], cycles=4000, aliases=[(8, 0)] if before else (),
        )[-1:]

    def force_part(p, source, before=(), span=None):
        span = span or (0, len(parts[p].lists))
        final = [floats(*grid[:2], 3, grid[2], slots), floats(*grid, slots)]
        return call(
            f"force_{p}", functools.partial(force_kernel, grid, parts[p], p, span),
            [numbers[0], *packs[p], wide, wide_state, source, *before],
            [spread(4)] + (final if p == 3 else []),
            [side_space(p, 4)], cycles=5000, aliases=[(9, 0)] if before else (),
        )[-2:]

    early = []

    def keep(run):
        def beside():
            early[:] = run()
            return tuple(early)

        return beside

    layers, one, two, _ = exchange(
        own.reshape(grid + (8, slots)), lambda: (wide,), keep(lambda: volume_part(0, own))
    )
    (volume,) = volume_part(3, two, volume_part(2, one, volume_part(1, layers, early)))

    layers, one, two, _ = exchange(
        volume.reshape(grid + (1, slots)),
        keep(lambda: density_part(0, volume, span=(0, cut))),
        keep(lambda: density_part(0, volume, early, span=(cut, leaves))),
    )
    acc = density_part(2, one, density_part(1, layers, early))
    (state,) = density_part(3, two, acc, [own, volume, energy])

    wide_state = call(
        "widen_state", functools.partial(widen_kernel, (0, 1, 2)), [state],
        [floats(leaves, 3, slots, slots)], cycles=1000,
    )[0]
    layers, one, two, _ = exchange(
        state.reshape(grid + (4, slots)),
        keep(lambda: force_part(0, state, span=(0, cut))),
        keep(lambda: force_part(0, state, early, span=(cut, leaves))),
    )
    push, heat = force_part(3, two, force_part(2, one, force_part(1, layers, early)))
    return jnp.swapaxes(push, 2, 3), heat


def solution(mesh):
    placed = (
        P("gx", "gy", "gz", None, None),
        P("gx", "gy", "gz", None, None),
        P("gx", "gy", "gz", None),
        P("gx", "gy", "gz", None),
        P("gx", "gy", "gz", None),
        P("gx", "gy", "gz"),
    )
    return jax.shard_map(
        shards,
        mesh=mesh,
        in_specs=placed,
        out_specs=(P("gx", "gy", "gz", None, None), P("gx", "gy", "gz", None)),
        check_vma=False,
    )
```

```python
import functools
import itertools

import jax
import jax.numpy as jnp
from jax import lax
from jax.experimental import pallas as pl
from jax.experimental.pallas import tpu as pltpu
from jax.sharding import PartitionSpec as P

AXES = (("gx", 0), ("gy", 1), ("gz", 2))
FAR = 1024.0
TINY = 1e-30
ROOM = 6 << 20
GROUP = 4
WIDE = (0, 1, 2, 4, 5, 6)
OFFSETS = tuple(itertools.product((-1, 0, 1), repeat=3))


def ends_of(block, axis, dim):
    count = lax.axis_size(axis)
    size = block.shape[dim]
    last = lax.slice_in_dim(block, size - 1, None, axis=dim)
    first = lax.slice_in_dim(block, 0, 1, axis=dim)
    if count == 1:
        return first, last, True
    if count == 2:
        ends = block if size == 2 else jnp.concatenate([first, last], axis=dim)
        ends = lax.ppermute(ends, axis, [(0, 1), (1, 0)])
        return lax.slice_in_dim(ends, 0, 1, axis=dim), lax.slice_in_dim(ends, 1, 2, axis=dim), True
    if count % 2:
        forward = [(i, (i + 1) % count) for i in range(count)]
        backward = [(target, source) for source, target in forward]
        return lax.ppermute(first, axis, backward), lax.ppermute(last, axis, forward), True
    even = lax.axis_index(axis) % 2 == 0
    near_pairs = [(i, i + 1 - 2 * (i % 2)) for i in range(count)]
    far_pairs = [(i, (i - 1 + 2 * (i % 2)) % count) for i in range(count)]
    one = lax.ppermute(jnp.where(even, last, first), axis, near_pairs)
    two = lax.ppermute(jnp.where(even, first, last), axis, far_pairs)
    return one, two, even


def low_and_high(block, axis, dim):
    one, two, one_is_high = ends_of(block, axis, dim)
    if one_is_high is True:
        return two, one
    return jnp.where(one_is_high, two, one), jnp.where(one_is_high, one, two)


def after(block, *others):
    return lax.optimization_barrier((block,) + others)[0]


def exchange(block, beside_x, beside_y):
    low, high = low_and_high(block, "gx", 0)
    wide = jnp.concatenate([low, block, high], axis=0)
    first = beside_x()
    low, high = low_and_high(after(wide, *first), "gy", 1)
    layers = jnp.concatenate([low, wide, high], axis=1)
    second = beside_y()
    one, two, one_is_high = ends_of(after(layers, *second), "gz", 2)
    return flat(layers), flat(one), flat(two), one_is_high


def column_constant(values, rows):
    ids = lax.broadcasted_iota(jnp.int32, (rows, 128), 0)
    out = jnp.zeros((rows, 128), jnp.float32)
    for row, value in enumerate(values):
        if value != 0.0:
            out = jnp.where(ids == row, jnp.float32(value), out)
    return out


def apart(own, row):
    return own[0] - row(0), own[1] - row(1), own[2] - row(2)


def volume_pair(own, row, keep):
    dx, dy, dz = apart(own, row)
    square = dx * dx + dy * dy + dz * dz
    radius = square * lax.rsqrt(jnp.maximum(square, TINY))
    inside = jnp.maximum(1.0 - radius, 0.0)
    keep[...] = inside
    second = inside * inside
    return ((second * second) * (1.25 - inside),)


def density_pair(own, row, kept):
    dx, dy, dz = apart(own, row)
    inside = kept[...]
    third = inside * inside * inside
    value = third * (inside * (1.25 - inside))
    relative = (row(4) - own[4]) * dx + (row(5) - own[5]) * dy + (row(6) - own[6]) * dz
    volume = row(7)
    return (
        row(3) * value,
        volume * value,
        (volume * third) * relative,
    )


def force_pair(own, row, kept):
    dx, dy, dz = apart(own, row)
    inside = kept[...]
    scaled = row(3) * (inside * inside * inside)
    relative = (own[4] - row(4)) * dx + (own[5] - row(5)) * dy + (own[6] - row(6)) * dz
    half = (own[10] + row(10)) / (own[8] + row(8))
    heat = own[9] + half
    push = (heat + (row(9) + half)) * scaled
    return (
        push * dx,
        push * dy,
        push * dz,
        (heat * scaled) * relative,
    )


def prepare_kernel(*refs):
    sources, out_ref, holds, sems = refs[:4], refs[4], refs[5:9], refs[9]
    copies = [
        pltpu.make_async_copy(source, hold, sems.at[i])
        for i, (source, hold) in enumerate(zip(sources, holds))
    ]
    for copy in copies:
        copy.start()
    for copy in copies:
        copy.wait()
    counts_ref, offsets_ref, velocity_ref, mass_ref = holds
    nx, ny, nz = mass_ref.shape[:3]
    for leaf, (x, y, z) in enumerate(itertools.product(range(nx), range(ny), range(nz))):
        for c in range(3):
            out_ref[leaf, c : c + 1, :] = offsets_ref[x, y, c, z : z + 1, :]
            out_ref[leaf, 4 + c : 5 + c, :] = velocity_ref[x, y, c, z : z + 1, :]
        out_ref[leaf, 3:4, :] = mass_ref[x, y, z : z + 1, :]
        number = counts_ref[x, y : y + 1, z : z + 1].astype(jnp.float32)
        out_ref[leaf, 7:8, :] = jnp.broadcast_to(number, (1, mass_ref.shape[3]))


def partners(grid):
    nx, ny, nz = grid
    parts = ([], [])
    for x, y, z in itertools.product(range(nx), range(ny), range(nz)):
        for part in parts:
            part.append([])
        for k, (ox, oy, oz) in enumerate(OFFSETS):
            tx, ty, tz = x + ox, y + oy, z + oz
            if 0 <= tz < nz:
                if 0 <= tx < nx and 0 <= ty < ny:
                    parts[0][-1].append((k, (tx * ny + ty) * nz + tz))
                else:
                    parts[1][-1].append((k, ((tx + 1) * (ny + 2) + ty + 1) * nz + tz))
    return parts


class Layers:
    def __init__(self, grid, part):
        self.lists = part
        self.mask_count = 27 * len(part)

    def bind(self, flag):
        self.moves = [column_constant(offset, 8) for offset in OFFSETS]

    def leaf(self, index):
        return index

    def mask_at(self, index, k):
        return index * 27 + k

    def move(self, k):
        return self.moves[k]


class Side:
    def __init__(self, grid, when):
        nx, ny, nz = grid
        self.depth, self.when = nz, when
        self.mask_count = 27 * nx * ny * nz
        columns = [(k, OFFSETS[k][:2]) for k in range(1, 27, 3)]
        self.lists = [
            [(k, (x + ox + 1) * (ny + 2) + y + oy + 1) for k, (ox, oy) in columns]
            for x, y in itertools.product(range(nx), range(ny))
        ]

    def bind(self, flag):
        self.high = flag if self.when else 1 - flag
        heights = lax.broadcasted_iota(jnp.int32, (8, 128), 0)
        along = jnp.where(heights == 2, (2 * self.high - 1).astype(jnp.float32), 0.0)
        self.moves = {k: column_constant(OFFSETS[k][:2], 8) + along for k in range(1, 27, 3)}

    def leaf(self, index):
        return index * self.depth + self.high * (self.depth - 1)

    def mask_at(self, index, k):
        return self.leaf(index) * 27 + (2 * self.high - 1) + k

    def move(self, k):
        return self.moves[k]


def longest(lists):
    return max(len(found) for found in lists)


def list_tiles(lists):
    return longest(lists) + 2


def split_place(start):
    return start & 127, lax.shift_right_logical(start, 7)


def put(list_ref, leaf, shift, tile, block, lanes):
    rolled = pltpu.roll(block, shift, axis=1)
    pltpu.store(list_ref.at[leaf, tile], rolled, mask=lanes >= shift)
    list_ref[leaf, tile + 1] = rolled


def close(list_ref, leaf, shift, tile, tail, lanes):
    pltpu.store(list_ref.at[leaf, tile], tail, mask=lanes >= shift)


def lane_ids(rows):
    return lax.broadcasted_iota(jnp.int32, (rows, 128), 1)


def pack_places(part, mask_ref, counts_ref, source_ref, list_ref, start_ref, last_ref, all_ref, other_ref):
    stride = longest(part.lists) + 1
    for index, found in enumerate(part.lists):
        kept, other = jnp.int32(0), jnp.int32(0)
        for number, (k, place) in enumerate(found):
            start_ref[index * stride + number] = kept
            other_ref[index * stride + number] = other
            size = counts_ref[place]
            chosen = size * mask_ref[part.mask_at(index, k)]
            kept, other = kept + chosen, other + (size - chosen)
        start_ref[index * stride + len(found)] = kept
        last_ref[index] = split_place(kept + 127)[1]
        other_ref[index * stride + len(found)] = other
        all_ref[index] = split_place(kept + other + 127)[1]

    lanes = lane_ids(8)
    only_places = lax.broadcasted_iota(jnp.int32, (8, 128), 0) < 3
    far = column_constant((FAR, FAR, FAR), 8)
    for index, found in enumerate(part.lists):
        for number, (k, place) in enumerate(found):
            shift, tile = split_place(start_ref[index * stride + number])
            put(list_ref, index, shift, tile, source_ref[place] + part.move(k), lanes)
        kept = start_ref[index * stride + len(found)]
        for number, (k, place) in enumerate(found):
            shift, tile = split_place(kept + other_ref[index * stride + number])
            block = jnp.where(only_places, source_ref[place] + part.move(k), 0.0)
            put(list_ref, index, shift, tile, block, lanes)
        shift, tile = split_place(kept + other_ref[index * stride + len(found)])
        close(list_ref, index, shift, tile, far, lanes)


def pack_side(part, span, source_ref, side_ref, start_ref, tail):
    height = source_ref.shape[1]
    lanes = lane_ids(height)
    last = column_constant(tail, height)
    stride = longest(part.lists) + 1
    for index in range(*span):
        found = part.lists[index]
        for number, (_, place) in enumerate(found):
            shift, tile = split_place(start_ref[index * stride + number])
            put(side_ref, index, shift, tile, source_ref[place], lanes)
        shift, tile = split_place(start_ref[index * stride + len(found)])
        close(side_ref, index, shift, tile, last, lanes)


def widen_kernel(rows, block_ref, out_ref):
    for leaf in range(block_ref.shape[0]):
        for index, c in enumerate(rows):
            row = block_ref[leaf, c : c + 1, :]
            out_ref[leaf, index] = jnp.transpose(jnp.broadcast_to(row, (128, 128)))


def read_counts(source_ref, counts_ref):
    for place in range(source_ref.shape[0]):
        counts_ref[place] = source_ref[place, 7:8, :].astype(jnp.int32)[0, 0]


def run_pairs(part, span, pair, n_sums, counts_ref, tiles_ref, own_of, row_of, kept_ref, before_ref, acc_ref):
    zero = jnp.zeros((8, 128), jnp.float32)

    def leaf_step(index, carry):
        leaf = part.leaf(index)
        count = counts_ref[leaf]
        tiles = tiles_ref[index]

        def group_step(group, carry):
            places = [
                pl.ds(pl.multiple_of(group * (8 * GROUP) + 8 * chunk, 8), 8) for chunk in range(GROUP)
            ]
            owns = [own_of(leaf, at) for at in places]

            def add_tile(tile, sums):
                rows = {}

                def row(c):
                    if c not in rows:
                        rows[c] = jnp.broadcast_to(row_of(index, tile, c), (8, 128))
                    return rows[c]

                terms = [
                    pair(own, row, kept_ref.at[index, tile, at, :]) for own, at in zip(owns, places)
                ]
                return tuple(tuple(a + b for a, b in zip(old, new)) for old, new in zip(sums, terms))

            def two_tiles(step, sums):
                return add_tile(2 * step + 1, add_tile(2 * step, sums))

            start = tuple(
                tuple(zero if before_ref is None else before_ref[leaf, i, at, :] for i in range(n_sums))
                for at in places
            )
            sums = lax.fori_loop(0, lax.shift_right_logical(tiles, 1), two_tiles, start)
            sums = lax.fori_loop(0, tiles & 1, lambda _, sums: add_tile(tiles - 1, sums), sums)
            for at, total in zip(places, sums):
                for i in range(n_sums):
                    acc_ref[leaf, i, at, :] = total[i]
            return carry

        groups = lax.shift_right_logical(count + (8 * GROUP - 1), (8 * GROUP).bit_length() - 1)
        return lax.fori_loop(0, groups, group_step, carry)

    lax.fori_loop(*span, leaf_step, 0)


def lane_sums(blocks):
    rows = []
    left = lane_ids(128) < 64
    for i in range(0, len(blocks) - 1, 2):
        one, two = blocks[i : i + 2]
        both = jnp.where(left, one, two) + pltpu.roll(jnp.where(left, two, one), 64, axis=1)
        both = jnp.transpose(both)
        rows += [jnp.sum(half, axis=0, keepdims=True) for half in (both[:64], both[64:])]
    if len(blocks) % 2:
        rows.append(jnp.sum(jnp.transpose(blocks[-1]), axis=0, keepdims=True))
    return rows


def leaf_totals(grid, acc_ref, counts_ref):
    for leaf, index in enumerate(itertools.product(*map(range, grid))):
        sums = lane_sums([acc_ref[leaf, i] for i in range(acc_ref.shape[1])])
        yield index, leaf, sums, lax.broadcasted_iota(jnp.int32, (1, 128), 1) < counts_ref[leaf]


def own_reader(*pieces):
    def own_of(leaf, at):
        return {c: ref[leaf, i, at, :] for ref, channels in pieces for i, c in enumerate(channels)}

    return own_of


def row_reader(list_ref, side_ref=None, base=8):
    def row_of(leaf, at, c):
        if c < base:
            return list_ref[leaf, at, c : c + 1, :]
        return side_ref[leaf, at, c - base : c - base + 1, :]

    return row_of


def volume_kernel(grid, part, stage, *refs):
    refs = list(refs)
    numbers_ref = refs.pop(0) if stage else None
    mask_ref, source_ref, wide_ref = refs[:3]
    before_ref = refs[3] if stage else None
    acc_ref, counts_ref, list_ref, start_ref, last_ref, kept_ref = refs[4 if stage else 3 :][:6]
    all_ref, other_ref = refs[-2:]
    read_counts(source_ref, counts_ref)
    if numbers_ref is None:
        numbers_ref = counts_ref
        numbers_ref[source_ref.shape[0]] = mask_ref[part.mask_count]
    part.bind(mask_ref[part.mask_count])
    pack_places(part, mask_ref, counts_ref, source_ref, list_ref, start_ref, last_ref, all_ref, other_ref)
    run_pairs(
        part, (0, len(part.lists)), volume_pair, 1, numbers_ref, all_ref,
        own_reader((wide_ref, WIDE)), row_reader(list_ref), kept_ref, before_ref, acc_ref,
    )
    if stage == 3:
        out_ref = refs[-3]
        for index, leaf, sums, valid in leaf_totals(grid, acc_ref, numbers_ref):
            out_ref[leaf] = jnp.where(valid, 1.0 / (1.0 + 4.0 * sums[0]), 1.0)


def density_kernel(grid, part, stage, span, *refs):
    numbers_ref, list_ref, start_ref, last_ref, kept_ref, wide_ref, source_ref = refs[:7]
    before_ref = refs[7] if stage or span[0] else None
    acc_ref = refs[11 if stage == 3 else 8 if before_ref is not None else 7]
    side_ref = refs[-1]
    part.bind(numbers_ref[numbers_ref.shape[0] - 1])
    pack_side(part, span, source_ref, side_ref, start_ref, ())
    run_pairs(
        part, span, density_pair, 3, numbers_ref, last_ref, own_reader((wide_ref, WIDE)),
        row_reader(list_ref, side_ref, 7), kept_ref, before_ref if stage else None, acc_ref,
    )
    if stage == 3:
        own_ref, volume_ref, energy_ref = refs[8:11]
        out_ref = refs[12]
        for (x, y, z), leaf, sums, valid in leaf_totals(grid, acc_ref, numbers_ref):
            density = (own_ref[leaf, 3:4, :] + 4.0 * sums[0]) / (volume_ref[leaf] + 4.0 * sums[1])
            density = jnp.where(valid, density, 1.0)
            energy = energy_ref[x, y, z : z + 1, :]
            out_ref[leaf, 0:1, :] = density
            out_ref[leaf, 1:2, :] = jnp.where(valid, (2.0 / 3.0) * energy / density, 0.0)
            out_ref[leaf, 2:3, :] = jnp.where(valid, jnp.maximum(20.0 * sums[2], 0.0), 0.0)
            out_ref[leaf, 3:4, :] = jnp.zeros_like(density)


def force_kernel(grid, part, stage, span, *refs):
    numbers_ref, list_ref, start_ref, last_ref, kept_ref, wide_ref, state_ref, source_ref = refs[:8]
    before_ref = refs[8] if stage or span[0] else None
    acc_ref = refs[9 if before_ref is not None else 8]
    side_ref = refs[-1]
    part.bind(numbers_ref[numbers_ref.shape[0] - 1])
    pack_side(part, span, source_ref, side_ref, start_ref, (1.0,))
    run_pairs(
        part, span, force_pair, 4, numbers_ref, last_ref,
        own_reader((wide_ref, WIDE), (state_ref, (8, 9, 10))), row_reader(list_ref, side_ref),
        kept_ref, before_ref if stage else None, acc_ref,
    )
    if stage == 3:
        push_ref, heat_ref = refs[10:12]
        for (x, y, z), leaf, sums, valid in leaf_totals(grid, acc_ref, numbers_ref):
            for c in range(3):
                push_ref[x, y, c, z : z + 1, :] = jnp.where(valid, 20.0 * sums[c], 0.0)
            heat_ref[x, y, z : z + 1, :] = jnp.where(valid, -20.0 * sums[3], 0.0)


def call(name, body, inputs, outs, scratch=(), cycles=0, aliases=()):
    def spec(x):
        scalar = x.dtype == jnp.int32 and len(x.shape) == 1
        return pl.BlockSpec(memory_space=pltpu.SMEM if scalar else pltpu.VMEM)

    return pl.pallas_call(
        body,
        out_shape=outs,
        in_specs=[spec(x) for x in inputs],
        out_specs=[spec(x) for x in outs],
        scratch_shapes=scratch,
        input_output_aliases=dict(aliases),
        compiler_params=pltpu.CompilerParams(vmem_limit_bytes=ROOM),
        cost_estimate=pl.CostEstimate(flops=cycles * 4096, bytes_accessed=1 << 20, transcendentals=0),
        name=name,
    )(*inputs)


def floats(*shape):
    return jax.ShapeDtypeStruct(shape, jnp.float32)


def integers(*shape):
    return jax.ShapeDtypeStruct(shape, jnp.int32)


def flat(block):
    return block.reshape((-1,) + block.shape[3:])


def shards(offsets, velocity, mass, energy, partner_mask, counts):
    grid = counts.shape
    slots = offsets.shape[4]
    assert slots == 128
    leaves = grid[0] * grid[1] * grid[2]
    parts = [Layers(grid, part) for part in partners(grid)] + [Side(grid, True), Side(grid, False)]
    inputs = [counts, jnp.swapaxes(offsets, 2, 3), jnp.swapaxes(velocity, 2, 3), mass]
    inputs = [pltpu.with_memory_space_constraint(x, pltpu.HBM) for x in inputs]
    own = pl.pallas_call(
        prepare_kernel,
        out_shape=floats(leaves, 8, slots),
        in_specs=[pl.BlockSpec(memory_space=pltpu.HBM)] * 4,
        out_specs=pl.BlockSpec(memory_space=pltpu.VMEM),
        scratch_shapes=[pltpu.VMEM(x.shape, x.dtype) for x in inputs] + [pltpu.SemaphoreType.DMA((4,))],
        compiler_params=pltpu.CompilerParams(vmem_limit_bytes=ROOM),
        name="prepare",
    )(*inputs)
    one_is_high = jnp.ones((1,), jnp.int32)
    if lax.axis_size("gz") > 2 and lax.axis_size("gz") % 2 == 0:
        one_is_high = 1 - lax.axis_index("gz").astype(jnp.int32)[None] % 2
    mask = jnp.concatenate([partner_mask.reshape(-1), one_is_high])
    wide = call(
        "widen", functools.partial(widen_kernel, WIDE), [own],
        [floats(leaves, len(WIDE), slots, slots)], cycles=2000,
    )[0]

    cut = 3 * leaves // 8

    def side_space(p, height):
        lists = parts[p].lists
        return pltpu.VMEM((len(lists), list_tiles(lists), height, slots), jnp.float32)

    def spread(n_sums):
        return floats(leaves, n_sums, slots, slots)

    def list_outs(p):
        lists = parts[p].lists
        count, tiles = len(lists), list_tiles(lists)
        return [
            floats(count, tiles, 8, slots), integers(count * (longest(lists) + 1)), integers(count),
            floats(count, tiles, slots, slots),
        ]

    numbers, packs = [], []

    def volume_part(p, source, before=()):
        inputs = numbers[:1] + [mask, source, wide, *before]
        outs = [spread(1), integers(source.shape[0] + (p == 0))] + list_outs(p)
        acc, number, *packed = call(
            f"volume_{p}", functools.partial(volume_kernel, grid, parts[p], p), inputs,
            outs + ([floats(leaves, 1, slots)] if p == 3 else []),
            [
                pltpu.SMEM((len(parts[p].lists),), jnp.int32),
                pltpu.SMEM((len(parts[p].lists) * (longest(parts[p].lists) + 1),), jnp.int32),
            ],
            cycles=3000,
            aliases=[(len(inputs) - 1, 0)] if before else (),
        )
        numbers.append(number)
        packs.append(packed[:4])
        return [packed[4] if p == 3 else acc]

    def density_part(p, source, before=(), more=(), span=None):
        span = span or (0, len(parts[p].lists))
        return call(
            f"density_{p}", functools.partial(density_kernel, grid, parts[p], p, span),
            [numbers[0], *packs[p], wide, source, *before, *more],
            [spread(3)] + ([floats(leaves, 4, slots)] if p == 3 else []),
            [side_space(p, 1)], cycles=4000, aliases=[(7, 0)] if before else (),
        )[-1:]

    def force_part(p, source, before=(), span=None):
        span = span or (0, len(parts[p].lists))
        final = [floats(*grid[:2], 3, grid[2], slots), floats(*grid, slots)]
        return call(
            f"force_{p}", functools.partial(force_kernel, grid, parts[p], p, span),
            [numbers[0], *packs[p], wide, wide_state, source, *before],
            [spread(4)] + (final if p == 3 else []),
            [side_space(p, 4)], cycles=5000, aliases=[(8, 0)] if before else (),
        )[-2:]

    early = []

    def keep(run):
        def beside():
            early[:] = run()
            return tuple(early)

        return beside

    layers, one, two, _ = exchange(
        own.reshape(grid + (8, slots)), lambda: (wide,), keep(lambda: volume_part(0, own))
    )
    (volume,) = volume_part(3, two, volume_part(2, one, volume_part(1, layers, early)))

    layers, one, two, _ = exchange(
        volume.reshape(grid + (1, slots)),
        keep(lambda: density_part(0, volume, span=(0, cut))),
        keep(lambda: density_part(0, volume, early, span=(cut, leaves))),
    )
    acc = density_part(2, one, density_part(1, layers, early))
    (state,) = density_part(3, two, acc, [own, volume, energy])

    wide_state = call(
        "widen_state", functools.partial(widen_kernel, (0, 1, 2)), [state],
        [floats(leaves, 3, slots, slots)], cycles=1000,
    )[0]
    layers, one, two, _ = exchange(
        state.reshape(grid + (4, slots)),
        keep(lambda: force_part(0, state, span=(0, cut))),
        keep(lambda: force_part(0, state, early, span=(cut, leaves))),
    )
    push, heat = force_part(3, two, force_part(2, one, force_part(1, layers, early)))
    return jnp.swapaxes(push, 2, 3), heat


def solution(mesh):
    placed = (
        P("gx", "gy", "gz", None, None),
        P("gx", "gy", "gz", None, None),
        P("gx", "gy", "gz", None),
        P("gx", "gy", "gz", None),
        P("gx", "gy", "gz", None),
        P("gx", "gy", "gz"),
    )
    return jax.shard_map(
        shards,
        mesh=mesh,
        in_specs=placed,
        out_specs=(P("gx", "gy", "gz", None, None), P("gx", "gy", "gz", None)),
        check_vma=False,
    )
```

```python
import functools
import itertools

import jax
import jax.numpy as jnp
from jax import lax
from jax.experimental import pallas as pl
from jax.experimental.pallas import tpu as pltpu
from jax.sharding import PartitionSpec as P

AXES = (("gx", 0), ("gy", 1), ("gz", 2))
FAR = 1024.0
TINY = 1e-30
ROOM = 6 << 20
GROUP = 4
WIDE = (0, 1, 2, 4, 5, 6)
OFFSETS = tuple(itertools.product((-1, 0, 1), repeat=3))


def ends_of(block, axis, dim):
    count = lax.axis_size(axis)
    size = block.shape[dim]
    last = lax.slice_in_dim(block, size - 1, None, axis=dim)
    first = lax.slice_in_dim(block, 0, 1, axis=dim)
    if count == 1:
        return first, last, True
    if count == 2:
        ends = block if size == 2 else jnp.concatenate([first, last], axis=dim)
        ends = lax.ppermute(ends, axis, [(0, 1), (1, 0)])
        return lax.slice_in_dim(ends, 0, 1, axis=dim), lax.slice_in_dim(ends, 1, 2, axis=dim), True
    if count % 2:
        forward = [(i, (i + 1) % count) for i in range(count)]
        backward = [(target, source) for source, target in forward]
        return lax.ppermute(first, axis, backward), lax.ppermute(last, axis, forward), True
    even = lax.axis_index(axis) % 2 == 0
    near_pairs = [(i, i + 1 - 2 * (i % 2)) for i in range(count)]
    far_pairs = [(i, (i - 1 + 2 * (i % 2)) % count) for i in range(count)]
    one = lax.ppermute(jnp.where(even, last, first), axis, near_pairs)
    two = lax.ppermute(jnp.where(even, first, last), axis, far_pairs)
    return one, two, even


def low_and_high(block, axis, dim):
    one, two, one_is_high = ends_of(block, axis, dim)
    if one_is_high is True:
        return two, one
    return jnp.where(one_is_high, two, one), jnp.where(one_is_high, one, two)


def after(block, *others):
    return lax.optimization_barrier((block,) + others)[0]


def exchange(block, beside_x, beside_y):
    low, high = low_and_high(block, "gx", 0)
    wide = jnp.concatenate([low, block, high], axis=0)
    first = beside_x()
    low, high = low_and_high(after(wide, *first), "gy", 1)
    layers = jnp.concatenate([low, wide, high], axis=1)
    second = beside_y()
    one, two, one_is_high = ends_of(after(layers, *second), "gz", 2)
    return flat(layers), flat(one), flat(two), one_is_high


def column_constant(values, rows):
    ids = lax.broadcasted_iota(jnp.int32, (rows, 128), 0)
    out = jnp.zeros((rows, 128), jnp.float32)
    for row, value in enumerate(values):
        if value != 0.0:
            out = jnp.where(ids == row, jnp.float32(value), out)
    return out


def apart(own, row):
    return own[0] - row(0), own[1] - row(1), own[2] - row(2)


def volume_pair(own, row, keep):
    dx, dy, dz = apart(own, row)
    square = dx * dx + dy * dy + dz * dz
    radius = square * lax.rsqrt(jnp.maximum(square, TINY))
    inside = jnp.maximum(1.0 - radius, 0.0)
    keep[...] = inside
    second = inside * inside
    return ((second * second) * (1.25 - inside),)


def density_pair(own, row, kept):
    dx, dy, dz = apart(own, row)
    inside = kept[...]
    third = inside * inside * inside
    value = third * (inside * (1.25 - inside))
    relative = (row(4) - own[4]) * dx + (row(5) - own[5]) * dy + (row(6) - own[6]) * dz
    volume = row(7)
    return (
        row(3) * value,
        volume * value,
        (volume * third) * relative,
    )


def force_pair(own, row, kept):
    dx, dy, dz = apart(own, row)
    inside = kept[...]
    scaled = row(3) * (inside * inside * inside)
    relative = (own[4] - row(4)) * dx + (own[5] - row(5)) * dy + (own[6] - row(6)) * dz
    half = (own[10] + row(10)) / (own[8] + row(8))
    heat = own[9] + half
    push = (heat + (row(9) + half)) * scaled
    return (
        push * dx,
        push * dy,
        push * dz,
        (heat * scaled) * relative,
    )


def prepare_kernel(*refs):
    sources, out_ref, holds, sems = refs[:4], refs[4], refs[5:9], refs[9]
    copies = [
        pltpu.make_async_copy(source, hold, sems.at[i])
        for i, (source, hold) in enumerate(zip(sources, holds))
    ]
    for copy in copies:
        copy.start()
    for copy in copies:
        copy.wait()
    counts_ref, offsets_ref, velocity_ref, mass_ref = holds
    nx, ny, nz = mass_ref.shape[:3]
    for leaf, (x, y, z) in enumerate(itertools.product(range(nx), range(ny), range(nz))):
        for c in range(3):
            out_ref[leaf, c : c + 1, :] = offsets_ref[x, y, c, z : z + 1, :]
            out_ref[leaf, 4 + c : 5 + c, :] = velocity_ref[x, y, c, z : z + 1, :]
        out_ref[leaf, 3:4, :] = mass_ref[x, y, z : z + 1, :]
        number = counts_ref[x, y : y + 1, z : z + 1].astype(jnp.float32)
        out_ref[leaf, 7:8, :] = jnp.broadcast_to(number, (1, mass_ref.shape[3]))


def partners(grid):
    nx, ny, nz = grid
    parts = ([], [])
    for x, y, z in itertools.product(range(nx), range(ny), range(nz)):
        for part in parts:
            part.append([])
        for k, (ox, oy, oz) in enumerate(OFFSETS):
            tx, ty, tz = x + ox, y + oy, z + oz
            if 0 <= tz < nz:
                if 0 <= tx < nx and 0 <= ty < ny:
                    parts[0][-1].append((k, (tx * ny + ty) * nz + tz))
                else:
                    parts[1][-1].append((k, ((tx + 1) * (ny + 2) + ty + 1) * nz + tz))
    return parts


class Layers:
    def __init__(self, grid, part):
        self.lists = part
        self.mask_count = 27 * len(part)

    def bind(self, flag):
        self.moves = [column_constant(offset, 8) for offset in OFFSETS]

    def leaf(self, index):
        return index

    def mask_at(self, index, k):
        return index * 27 + k

    def move(self, k):
        return self.moves[k]


class Side:
    def __init__(self, grid, when):
        nx, ny, nz = grid
        self.depth, self.when = nz, when
        self.mask_count = 27 * nx * ny * nz
        columns = [(k, OFFSETS[k][:2]) for k in range(1, 27, 3)]
        self.lists = [
            [(k, (x + ox + 1) * (ny + 2) + y + oy + 1) for k, (ox, oy) in columns]
            for x, y in itertools.product(range(nx), range(ny))
        ]

    def bind(self, flag):
        self.high = flag if self.when else 1 - flag
        heights = lax.broadcasted_iota(jnp.int32, (8, 128), 0)
        along = jnp.where(heights == 2, (2 * self.high - 1).astype(jnp.float32), 0.0)
        self.moves = {k: column_constant(OFFSETS[k][:2], 8) + along for k in range(1, 27, 3)}

    def leaf(self, index):
        return index * self.depth + self.high * (self.depth - 1)

    def mask_at(self, index, k):
        return self.leaf(index) * 27 + (2 * self.high - 1) + k

    def move(self, k):
        return self.moves[k]


def longest(lists):
    return max(len(found) for found in lists)


def list_tiles(lists):
    return longest(lists) + 2


def tile_of(start):
    return lax.shift_right_logical(start, 7)


def from_lane(start, lanes):
    return lanes >= (jnp.broadcast_to(start, lanes.shape) & 127)


def put(list_ref, index, start, block, lanes):
    tile = tile_of(start)
    rolled = pltpu.roll(block, start, axis=1)
    pltpu.store(list_ref.at[index, tile], rolled, mask=from_lane(start, lanes))
    list_ref[index, tile + 1] = rolled


def close(list_ref, index, start, tail, lanes):
    pltpu.store(list_ref.at[index, tile_of(start)], tail, mask=from_lane(start, lanes))


def lane_ids(rows):
    return lax.broadcasted_iota(jnp.int32, (rows, 128), 1)


def pack_places(part, mask_ref, counts_ref, source_ref, list_ref, start_ref, last_ref, all_ref, other_ref):
    stride = longest(part.lists) + 1
    for index, found in enumerate(part.lists):
        kept, other = jnp.int32(0), jnp.int32(0)
        for number, (k, place) in enumerate(found):
            start_ref[index * stride + number] = kept
            other_ref[index * stride + number] = other
            size = counts_ref[place]
            chosen = size * mask_ref[part.mask_at(index, k)]
            kept, other = kept + chosen, other + (size - chosen)
        start_ref[index * stride + len(found)] = kept
        last_ref[index] = tile_of(kept + 127)
        other_ref[index * stride + len(found)] = other
        all_ref[index] = tile_of(kept + other + 127)

    lanes = lane_ids(8)
    only_places = lax.broadcasted_iota(jnp.int32, (8, 128), 0) < 3
    far = column_constant((FAR, FAR, FAR), 8)
    for index, found in enumerate(part.lists):
        for number, (k, place) in enumerate(found):
            put(list_ref, index, start_ref[index * stride + number], source_ref[place] + part.move(k), lanes)
        kept = start_ref[index * stride + len(found)]
        for number, (k, place) in enumerate(found):
            block = jnp.where(only_places, source_ref[place] + part.move(k), 0.0)
            put(list_ref, index, kept + other_ref[index * stride + number], block, lanes)
        close(list_ref, index, kept + other_ref[index * stride + len(found)], far, lanes)


def pack_side(part, span, source_ref, side_ref, start_ref, tail):
    height = source_ref.shape[1]
    lanes = lane_ids(height)
    last = column_constant(tail, height)
    stride = longest(part.lists) + 1
    for index in range(*span):
        found = part.lists[index]
        for number, (_, place) in enumerate(found):
            put(side_ref, index, start_ref[index * stride + number], source_ref[place], lanes)
        close(side_ref, index, start_ref[index * stride + len(found)], last, lanes)


def widen_kernel(rows, block_ref, out_ref):
    for leaf in range(block_ref.shape[0]):
        for index, c in enumerate(rows):
            row = block_ref[leaf, c : c + 1, :]
            out_ref[leaf, index] = jnp.transpose(jnp.broadcast_to(row, (128, 128)))


def read_counts(source_ref, counts_ref):
    for place in range(source_ref.shape[0]):
        counts_ref[place] = source_ref[place, 7:8, :].astype(jnp.int32)[0, 0]


def run_pairs(part, span, pair, n_sums, counts_ref, tiles_ref, own_of, row_of, kept_ref, before_ref, acc_ref):
    zero = jnp.zeros((8, 128), jnp.float32)

    def leaf_step(index, carry):
        leaf = part.leaf(index)
        count = counts_ref[leaf]
        tiles = tiles_ref[index]

        def group_step(group, carry):
            places = [
                pl.ds(pl.multiple_of(group * (8 * GROUP) + 8 * chunk, 8), 8) for chunk in range(GROUP)
            ]
            owns = [own_of(leaf, at) for at in places]

            def add_tile(tile, sums):
                rows = {}

                def row(c):
                    if c not in rows:
                        rows[c] = jnp.broadcast_to(row_of(index, tile, c), (8, 128))
                    return rows[c]

                terms = [
                    pair(own, row, kept_ref.at[index, tile, at, :]) for own, at in zip(owns, places)
                ]
                return tuple(tuple(a + b for a, b in zip(old, new)) for old, new in zip(sums, terms))

            def two_tiles(step, sums):
                return add_tile(2 * step + 1, add_tile(2 * step, sums))

            start = tuple(
                tuple(zero if before_ref is None else before_ref[leaf, i, at, :] for i in range(n_sums))
                for at in places
            )
            sums = lax.fori_loop(0, lax.shift_right_logical(tiles, 1), two_tiles, start)
            sums = lax.fori_loop(0, tiles & 1, lambda _, sums: add_tile(tiles - 1, sums), sums)
            for at, total in zip(places, sums):
                for i in range(n_sums):
                    acc_ref[leaf, i, at, :] = total[i]
            return carry

        groups = lax.shift_right_logical(count + (8 * GROUP - 1), (8 * GROUP).bit_length() - 1)
        return lax.fori_loop(0, groups, group_step, carry)

    lax.fori_loop(*span, leaf_step, 0)


def lane_sums(blocks):
    return [jnp.sum(jnp.transpose(block), axis=0, keepdims=True) for block in blocks]


def leaf_totals(grid, acc_ref, counts_ref):
    for leaf, index in enumerate(itertools.product(*map(range, grid))):
        sums = lane_sums([acc_ref[leaf, i] for i in range(acc_ref.shape[1])])
        yield index, leaf, sums, lax.broadcasted_iota(jnp.int32, (1, 128), 1) < counts_ref[leaf]


def own_reader(*pieces):
    def own_of(leaf, at):
        return {c: ref[leaf, i, at, :] for ref, channels in pieces for i, c in enumerate(channels)}

    return own_of


def row_reader(list_ref, side_ref=None, base=8):
    def row_of(leaf, at, c):
        if c < base:
            return list_ref[leaf, at, c : c + 1, :]
        return side_ref[leaf, at, c - base : c - base + 1, :]

    return row_of


def volume_kernel(grid, part, stage, *refs):
    refs = list(refs)
    numbers_ref = refs.pop(0) if stage else None
    mask_ref, source_ref, wide_ref = refs[:3]
    before_ref = refs[3] if stage else None
    acc_ref, counts_ref, list_ref, start_ref, last_ref, kept_ref = refs[4 if stage else 3 :][:6]
    all_ref, other_ref = refs[-2:]
    read_counts(source_ref, counts_ref)
    if numbers_ref is None:
        numbers_ref = counts_ref
        numbers_ref[source_ref.shape[0]] = mask_ref[part.mask_count]
    part.bind(mask_ref[part.mask_count])
    pack_places(part, mask_ref, counts_ref, source_ref, list_ref, start_ref, last_ref, all_ref, other_ref)
    run_pairs(
        part, (0, len(part.lists)), volume_pair, 1, numbers_ref, all_ref,
        own_reader((wide_ref, WIDE)), row_reader(list_ref), kept_ref, before_ref, acc_ref,
    )
    if stage == 3:
        out_ref = refs[-3]
        for index, leaf, sums, valid in leaf_totals(grid, acc_ref, numbers_ref):
            out_ref[leaf] = jnp.where(valid, 1.0 / (1.0 + 4.0 * sums[0]), 1.0)


def density_kernel(grid, part, stage, span, *refs):
    numbers_ref, list_ref, start_ref, last_ref, kept_ref, wide_ref, source_ref = refs[:7]
    before_ref = refs[7] if stage or span[0] else None
    acc_ref = refs[11 if stage == 3 else 8 if before_ref is not None else 7]
    side_ref = refs[-1]
    part.bind(numbers_ref[numbers_ref.shape[0] - 1])
    pack_side(part, span, source_ref, side_ref, start_ref, ())
    run_pairs(
        part, span, density_pair, 3, numbers_ref, last_ref, own_reader((wide_ref, WIDE)),
        row_reader(list_ref, side_ref, 7), kept_ref, before_ref if stage else None, acc_ref,
    )
    if stage == 3:
        own_ref, volume_ref, energy_ref = refs[8:11]
        out_ref = refs[12]
        for (x, y, z), leaf, sums, valid in leaf_totals(grid, acc_ref, numbers_ref):
            density = (own_ref[leaf, 3:4, :] + 4.0 * sums[0]) / (volume_ref[leaf] + 4.0 * sums[1])
            density = jnp.where(valid, density, 1.0)
            energy = energy_ref[x, y, z : z + 1, :]
            out_ref[leaf, 0:1, :] = density
            out_ref[leaf, 1:2, :] = jnp.where(valid, (2.0 / 3.0) * energy / density, 0.0)
            out_ref[leaf, 2:3, :] = jnp.where(valid, jnp.maximum(20.0 * sums[2], 0.0), 0.0)
            out_ref[leaf, 3:4, :] = jnp.zeros_like(density)


def force_kernel(grid, part, stage, span, *refs):
    numbers_ref, list_ref, start_ref, last_ref, kept_ref, wide_ref, state_ref, source_ref = refs[:8]
    before_ref = refs[8] if stage or span[0] else None
    acc_ref = refs[9 if before_ref is not None else 8]
    side_ref = refs[-1]
    part.bind(numbers_ref[numbers_ref.shape[0] - 1])
    pack_side(part, span, source_ref, side_ref, start_ref, (1.0,))
    run_pairs(
        part, span, force_pair, 4, numbers_ref, last_ref,
        own_reader((wide_ref, WIDE), (state_ref, (8, 9, 10))), row_reader(list_ref, side_ref),
        kept_ref, before_ref if stage else None, acc_ref,
    )
    if stage == 3:
        push_ref, heat_ref = refs[10:12]
        for (x, y, z), leaf, sums, valid in leaf_totals(grid, acc_ref, numbers_ref):
            for c in range(3):
                push_ref[x, y, c, z : z + 1, :] = jnp.where(valid, 20.0 * sums[c], 0.0)
            heat_ref[x, y, z : z + 1, :] = jnp.where(valid, -20.0 * sums[3], 0.0)


def call(name, body, inputs, outs, scratch=(), cycles=0, aliases=()):
    def spec(x):
        scalar = x.dtype == jnp.int32 and len(x.shape) == 1
        return pl.BlockSpec(memory_space=pltpu.SMEM if scalar else pltpu.VMEM)

    return pl.pallas_call(
        body,
        out_shape=outs,
        in_specs=[spec(x) for x in inputs],
        out_specs=[spec(x) for x in outs],
        scratch_shapes=scratch,
        input_output_aliases=dict(aliases),
        compiler_params=pltpu.CompilerParams(vmem_limit_bytes=ROOM),
        cost_estimate=pl.CostEstimate(flops=cycles * 4096, bytes_accessed=1 << 20, transcendentals=0),
        name=name,
    )(*inputs)


def floats(*shape):
    return jax.ShapeDtypeStruct(shape, jnp.float32)


def integers(*shape):
    return jax.ShapeDtypeStruct(shape, jnp.int32)


def flat(block):
    return block.reshape((-1,) + block.shape[3:])


def shards(offsets, velocity, mass, energy, partner_mask, counts):
    grid = counts.shape
    slots = offsets.shape[4]
    assert slots == 128
    leaves = grid[0] * grid[1] * grid[2]
    parts = [Layers(grid, part) for part in partners(grid)] + [Side(grid, True), Side(grid, False)]
    inputs = [counts, jnp.swapaxes(offsets, 2, 3), jnp.swapaxes(velocity, 2, 3), mass]
    inputs = [pltpu.with_memory_space_constraint(x, pltpu.HBM) for x in inputs]
    own = pl.pallas_call(
        prepare_kernel,
        out_shape=floats(leaves, 8, slots),
        in_specs=[pl.BlockSpec(memory_space=pltpu.HBM)] * 4,
        out_specs=pl.BlockSpec(memory_space=pltpu.VMEM),
        scratch_shapes=[pltpu.VMEM(x.shape, x.dtype) for x in inputs] + [pltpu.SemaphoreType.DMA((4,))],
        compiler_params=pltpu.CompilerParams(vmem_limit_bytes=ROOM),
        name="prepare",
    )(*inputs)
    one_is_high = jnp.ones((1,), jnp.int32)
    if lax.axis_size("gz") > 2 and lax.axis_size("gz") % 2 == 0:
        one_is_high = 1 - lax.axis_index("gz").astype(jnp.int32)[None] % 2
    mask = jnp.concatenate([partner_mask.reshape(-1), one_is_high])
    wide = call(
        "widen", functools.partial(widen_kernel, WIDE), [own],
        [floats(leaves, len(WIDE), slots, slots)], cycles=2000,
    )[0]

    cut = 3 * leaves // 8

    def side_space(p, height):
        lists = parts[p].lists
        return pltpu.VMEM((len(lists), list_tiles(lists), height, slots), jnp.float32)

    def spread(n_sums):
        return floats(leaves, n_sums, slots, slots)

    def list_outs(p):
        lists = parts[p].lists
        count, tiles = len(lists), list_tiles(lists)
        return [
            floats(count, tiles, 8, slots), integers(count * (longest(lists) + 1)), integers(count),
            floats(count, tiles, slots, slots),
        ]

    numbers, packs = [], []

    def volume_part(p, source, before=()):
        inputs = numbers[:1] + [mask, source, wide, *before]
        outs = [spread(1), integers(source.shape[0] + (p == 0))] + list_outs(p)
        acc, number, *packed = call(
            f"volume_{p}", functools.partial(volume_kernel, grid, parts[p], p), inputs,
            outs + ([floats(leaves, 1, slots)] if p == 3 else []),
            [
                pltpu.SMEM((len(parts[p].lists),), jnp.int32),
                pltpu.SMEM((len(parts[p].lists) * (longest(parts[p].lists) + 1),), jnp.int32),
            ],
            cycles=3000,
            aliases=[(len(inputs) - 1, 0)] if before else (),
        )
        numbers.append(number)
        packs.append(packed[:4])
        return [packed[4] if p == 3 else acc]

    def density_part(p, source, before=(), more=(), span=None):
        span = span or (0, len(parts[p].lists))
        return call(
            f"density_{p}", functools.partial(density_kernel, grid, parts[p], p, span),
            [numbers[0], *packs[p], wide, source, *before, *more],
            [spread(3)] + ([floats(leaves, 4, slots)] if p == 3 else []),
            [side_space(p, 1)], cycles=4000, aliases=[(7, 0)] if before else (),
        )[-1:]

    def force_part(p, source, before=(), span=None):
        span = span or (0, len(parts[p].lists))
        final = [floats(*grid[:2], 3, grid[2], slots), floats(*grid, slots)]
        return call(
            f"force_{p}", functools.partial(force_kernel, grid, parts[p], p, span),
            [numbers[0], *packs[p], wide, wide_state, source, *before],
            [spread(4)] + (final if p == 3 else []),
            [side_space(p, 4)], cycles=5000, aliases=[(8, 0)] if before else (),
        )[-2:]

    early = []

    def keep(run):
        def beside():
            early[:] = run()
            return tuple(early)

        return beside

    layers, one, two, _ = exchange(
        own.reshape(grid + (8, slots)), lambda: (wide,), keep(lambda: volume_part(0, own))
    )
    (volume,) = volume_part(3, two, volume_part(2, one, volume_part(1, layers, early)))

    layers, one, two, _ = exchange(
        volume.reshape(grid + (1, slots)),
        keep(lambda: density_part(0, volume, span=(0, cut))),
        keep(lambda: density_part(0, volume, early, span=(cut, leaves))),
    )
    acc = density_part(2, one, density_part(1, layers, early))
    (state,) = density_part(3, two, acc, [own, volume, energy])

    wide_state = call(
        "widen_state", functools.partial(widen_kernel, (0, 1, 2)), [state],
        [floats(leaves, 3, slots, slots)], cycles=1000,
    )[0]
    layers, one, two, _ = exchange(
        state.reshape(grid + (4, slots)),
        keep(lambda: force_part(0, state, span=(0, cut))),
        keep(lambda: force_part(0, state, early, span=(cut, leaves))),
    )
    push, heat = force_part(3, two, force_part(2, one, force_part(1, layers, early)))
    return jnp.swapaxes(push, 2, 3), heat


def solution(mesh):
    placed = (
        P("gx", "gy", "gz", None, None),
        P("gx", "gy", "gz", None, None),
        P("gx", "gy", "gz", None),
        P("gx", "gy", "gz", None),
        P("gx", "gy", "gz", None),
        P("gx", "gy", "gz"),
    )
    return jax.shard_map(
        shards,
        mesh=mesh,
        in_specs=placed,
        out_specs=(P("gx", "gy", "gz", None, None), P("gx", "gy", "gz", None)),
        check_vma=False,
    )
```

```python
import functools
import itertools

import jax
import jax.numpy as jnp
from jax import lax
from jax.experimental import pallas as pl
from jax.experimental.pallas import tpu as pltpu
from jax.sharding import PartitionSpec as P

AXES = (("gx", 0), ("gy", 1), ("gz", 2))
FAR = 1024.0
TINY = 1e-30
ROOM = 6 << 20
GROUP = 4
WIDE = (0, 1, 2, 4, 5, 6)
OFFSETS = tuple(itertools.product((-1, 0, 1), repeat=3))


def ends_of(block, axis, dim):
    count = lax.axis_size(axis)
    size = block.shape[dim]
    last = lax.slice_in_dim(block, size - 1, None, axis=dim)
    first = lax.slice_in_dim(block, 0, 1, axis=dim)
    if count == 1:
        return first, last, True
    if count == 2:
        ends = block if size == 2 else jnp.concatenate([first, last], axis=dim)
        ends = lax.ppermute(ends, axis, [(0, 1), (1, 0)])
        return lax.slice_in_dim(ends, 0, 1, axis=dim), lax.slice_in_dim(ends, 1, 2, axis=dim), True
    if count % 2:
        forward = [(i, (i + 1) % count) for i in range(count)]
        backward = [(target, source) for source, target in forward]
        return lax.ppermute(first, axis, backward), lax.ppermute(last, axis, forward), True
    even = lax.axis_index(axis) % 2 == 0
    near_pairs = [(i, i + 1 - 2 * (i % 2)) for i in range(count)]
    far_pairs = [(i, (i - 1 + 2 * (i % 2)) % count) for i in range(count)]
    one = lax.ppermute(jnp.where(even, last, first), axis, near_pairs)
    two = lax.ppermute(jnp.where(even, first, last), axis, far_pairs)
    return one, two, even


def low_and_high(block, axis, dim):
    one, two, one_is_high = ends_of(block, axis, dim)
    if one_is_high is True:
        return two, one
    return jnp.where(one_is_high, two, one), jnp.where(one_is_high, one, two)


def after(block, *others):
    return lax.optimization_barrier((block,) + others)[0]


def exchange(block, beside_x, beside_y):
    low, high = low_and_high(block, "gx", 0)
    wide = jnp.concatenate([low, block, high], axis=0)
    first = beside_x()
    low, high = low_and_high(after(wide, *first), "gy", 1)
    layers = jnp.concatenate([low, wide, high], axis=1)
    second = beside_y()
    one, two, one_is_high = ends_of(after(layers, *second), "gz", 2)
    return flat(layers), flat(one), flat(two), one_is_high


def column_constant(values, rows):
    ids = lax.broadcasted_iota(jnp.int32, (rows, 128), 0)
    out = jnp.zeros((rows, 128), jnp.float32)
    for row, value in enumerate(values):
        if value != 0.0:
            out = jnp.where(ids == row, jnp.float32(value), out)
    return out


def apart(own, row):
    return own[0] - row(0), own[1] - row(1), own[2] - row(2)


def volume_pair(own, row, keep):
    dx, dy, dz = apart(own, row)
    square = dx * dx + dy * dy + dz * dz
    radius = square * lax.rsqrt(jnp.maximum(square, TINY))
    inside = jnp.maximum(1.0 - radius, 0.0)
    keep[...] = inside
    second = inside * inside
    return ((second * second) * (1.25 - inside),)


def density_pair(own, row, kept):
    dx, dy, dz = apart(own, row)
    inside = kept[...]
    third = inside * inside * inside
    value = third * (inside * (1.25 - inside))
    relative = (row(4) - own[4]) * dx + (row(5) - own[5]) * dy + (row(6) - own[6]) * dz
    volume = row(7)
    return (
        row(3) * value,
        volume * value,
        (volume * third) * relative,
    )


def force_pair(own, row, kept):
    dx, dy, dz = apart(own, row)
    inside = kept[...]
    scaled = row(3) * (inside * inside * inside)
    relative = (own[4] - row(4)) * dx + (own[5] - row(5)) * dy + (own[6] - row(6)) * dz
    half = (own[10] + row(10)) / (own[8] + row(8))
    heat = own[9] + half
    push = (heat + (row(9) + half)) * scaled
    return (
        push * dx,
        push * dy,
        push * dz,
        (heat * scaled) * relative,
    )


def prepare_kernel(*refs):
    sources, out_ref, holds, sems = refs[:4], refs[4], refs[5:9], refs[9]
    copies = [
        pltpu.make_async_copy(source, hold, sems.at[i])
        for i, (source, hold) in enumerate(zip(sources, holds))
    ]
    for copy in copies:
        copy.start()
    for copy in copies:
        copy.wait()
    counts_ref, offsets_ref, velocity_ref, mass_ref = holds
    nx, ny, nz = mass_ref.shape[:3]
    for leaf, (x, y, z) in enumerate(itertools.product(range(nx), range(ny), range(nz))):
        for c in range(3):
            out_ref[leaf, c : c + 1, :] = offsets_ref[x, y, c, z : z + 1, :]
            out_ref[leaf, 4 + c : 5 + c, :] = velocity_ref[x, y, c, z : z + 1, :]
        out_ref[leaf, 3:4, :] = mass_ref[x, y, z : z + 1, :]
        number = counts_ref[x, y : y + 1, z : z + 1].astype(jnp.float32)
        out_ref[leaf, 7:8, :] = jnp.broadcast_to(number, (1, mass_ref.shape[3]))


def partners(grid):
    nx, ny, nz = grid
    parts = ([], [])
    for x, y, z in itertools.product(range(nx), range(ny), range(nz)):
        for part in parts:
            part.append([])
        for k, (ox, oy, oz) in enumerate(OFFSETS):
            tx, ty, tz = x + ox, y + oy, z + oz
            if 0 <= tz < nz:
                if 0 <= tx < nx and 0 <= ty < ny:
                    parts[0][-1].append((k, (tx * ny + ty) * nz + tz))
                else:
                    parts[1][-1].append((k, ((tx + 1) * (ny + 2) + ty + 1) * nz + tz))
    return parts


class Layers:
    def __init__(self, grid, part):
        self.lists = part
        self.mask_count = 27 * len(part)

    def bind(self, flag):
        self.moves = [column_constant(offset, 8) for offset in OFFSETS]

    def leaf(self, index):
        return index

    def mask_at(self, index, k):
        return index * 27 + k

    def move(self, k):
        return self.moves[k]


class Side:
    def __init__(self, grid, when):
        nx, ny, nz = grid
        self.depth, self.when = nz, when
        self.mask_count = 27 * nx * ny * nz
        columns = [(k, OFFSETS[k][:2]) for k in range(1, 27, 3)]
        self.lists = [
            [(k, (x + ox + 1) * (ny + 2) + y + oy + 1) for k, (ox, oy) in columns]
            for x, y in itertools.product(range(nx), range(ny))
        ]

    def bind(self, flag):
        self.high = flag if self.when else 1 - flag
        heights = lax.broadcasted_iota(jnp.int32, (8, 128), 0)
        along = jnp.where(heights == 2, (2 * self.high - 1).astype(jnp.float32), 0.0)
        self.moves = {k: column_constant(OFFSETS[k][:2], 8) + along for k in range(1, 27, 3)}

    def leaf(self, index):
        return index * self.depth + self.high * (self.depth - 1)

    def mask_at(self, index, k):
        return self.leaf(index) * 27 + (2 * self.high - 1) + k

    def move(self, k):
        return self.moves[k]


def longest(lists):
    return max(len(found) for found in lists)


def list_tiles(lists):
    return longest(lists) + 2


def tile_of(start):
    return lax.shift_right_logical(start, 7)


def from_lane(start, lanes):
    return lanes >= (jnp.broadcast_to(start, lanes.shape) & 127)


def put(list_ref, index, start, block, lanes):
    tile = tile_of(start)
    rolled = pltpu.roll(block, start, axis=1)
    pltpu.store(list_ref.at[index, tile], rolled, mask=from_lane(start, lanes))
    list_ref[index, tile + 1] = rolled


def close(list_ref, index, start, tail, lanes):
    pltpu.store(list_ref.at[index, tile_of(start)], tail, mask=from_lane(start, lanes))


def lane_ids(rows):
    return lax.broadcasted_iota(jnp.int32, (rows, 128), 1)


def pack_places(part, mask_ref, counts_ref, source_ref, list_ref, start_ref, last_ref, all_ref, other_ref):
    stride = longest(part.lists) + 1
    for index, found in enumerate(part.lists):
        kept, other = jnp.int32(0), jnp.int32(0)
        for number, (k, place) in enumerate(found):
            start_ref[index * stride + number] = kept
            other_ref[index * stride + number] = other
            size = counts_ref[place]
            chosen = size * mask_ref[part.mask_at(index, k)]
            kept, other = kept + chosen, other + (size - chosen)
        start_ref[index * stride + len(found)] = kept
        last_ref[index] = tile_of(kept + 127)
        other_ref[index * stride + len(found)] = other
        all_ref[index] = tile_of(kept + other + 127)

    lanes = lane_ids(8)
    only_places = lax.broadcasted_iota(jnp.int32, (8, 128), 0) < 3
    far = column_constant((FAR, FAR, FAR), 8)
    for index, found in enumerate(part.lists):
        for number, (k, place) in enumerate(found):
            put(list_ref, index, start_ref[index * stride + number], source_ref[place] + part.move(k), lanes)
        kept = start_ref[index * stride + len(found)]
        for number, (k, place) in enumerate(found):
            block = jnp.where(only_places, source_ref[place] + part.move(k), 0.0)
            put(list_ref, index, kept + other_ref[index * stride + number], block, lanes)
        close(list_ref, index, kept + other_ref[index * stride + len(found)], far, lanes)


def pack_side(part, span, source_ref, side_ref, start_ref, tail):
    height = source_ref.shape[1]
    lanes = lane_ids(height)
    last = column_constant(tail, height)
    stride = longest(part.lists) + 1
    for index in range(*span):
        found = part.lists[index]
        for number, (_, place) in enumerate(found):
            put(side_ref, index, start_ref[index * stride + number], source_ref[place], lanes)
        close(side_ref, index, start_ref[index * stride + len(found)], last, lanes)


def widen_kernel(rows, block_ref, out_ref):
    for leaf in range(block_ref.shape[0]):
        for index, c in enumerate(rows):
            row = block_ref[leaf, c : c + 1, :]
            out_ref[leaf, index] = jnp.transpose(jnp.broadcast_to(row, (128, 128)))


def read_counts(source_ref, counts_ref):
    for place in range(source_ref.shape[0]):
        counts_ref[place] = source_ref[place, 7:8, :].astype(jnp.int32)[0, 0]


def run_pairs(part, span, pair, n_sums, counts_ref, tiles_ref, own_of, row_of, kept_ref, before_ref, acc_ref, size=GROUP):
    zero = jnp.zeros((8, 128), jnp.float32)

    def leaf_step(index, carry):
        leaf = part.leaf(index)
        count = counts_ref[leaf]
        tiles = tiles_ref[index]

        def group_step(group, carry):
            places = [
                pl.ds(pl.multiple_of(group * (8 * size) + 8 * chunk, 8), 8) for chunk in range(size)
            ]
            owns = [own_of(leaf, at) for at in places]

            def add_tile(tile, sums):
                rows = {}

                def row(c):
                    if c not in rows:
                        rows[c] = jnp.broadcast_to(row_of(index, tile, c), (8, 128))
                    return rows[c]

                terms = [
                    pair(own, row, kept_ref.at[index, tile, at, :]) for own, at in zip(owns, places)
                ]
                return tuple(tuple(a + b for a, b in zip(old, new)) for old, new in zip(sums, terms))

            def two_tiles(step, sums):
                return add_tile(2 * step + 1, add_tile(2 * step, sums))

            start = tuple(
                tuple(zero if before_ref is None else before_ref[leaf, i, at, :] for i in range(n_sums))
                for at in places
            )
            sums = lax.fori_loop(0, lax.shift_right_logical(tiles, 1), two_tiles, start)
            sums = lax.fori_loop(0, tiles & 1, lambda _, sums: add_tile(tiles - 1, sums), sums)
            for at, total in zip(places, sums):
                for i in range(n_sums):
                    acc_ref[leaf, i, at, :] = total[i]
            return carry

        groups = lax.shift_right_logical(count + (8 * size - 1), (8 * size).bit_length() - 1)
        return lax.fori_loop(0, groups, group_step, carry)

    lax.fori_loop(*span, leaf_step, 0)


def lane_sums(blocks):
    return [jnp.sum(jnp.transpose(block), axis=0, keepdims=True) for block in blocks]


def leaf_totals(grid, acc_ref, counts_ref):
    for leaf, index in enumerate(itertools.product(*map(range, grid))):
        sums = lane_sums([acc_ref[leaf, i] for i in range(acc_ref.shape[1])])
        yield index, leaf, sums, lax.broadcasted_iota(jnp.int32, (1, 128), 1) < counts_ref[leaf]


def own_reader(*pieces):
    def own_of(leaf, at):
        return {c: ref[leaf, i, at, :] for ref, channels in pieces for i, c in enumerate(channels)}

    return own_of


def row_reader(list_ref, side_ref=None, base=8):
    def row_of(leaf, at, c):
        if c < base:
            return list_ref[leaf, at, c : c + 1, :]
        return side_ref[leaf, at, c - base : c - base + 1, :]

    return row_of


def volume_kernel(grid, part, stage, *refs):
    refs = list(refs)
    numbers_ref = refs.pop(0) if stage else None
    mask_ref, source_ref, wide_ref = refs[:3]
    before_ref = refs[3] if stage else None
    acc_ref, counts_ref, list_ref, start_ref, last_ref, kept_ref = refs[4 if stage else 3 :][:6]
    all_ref, other_ref = refs[-2:]
    read_counts(source_ref, counts_ref)
    if numbers_ref is None:
        numbers_ref = counts_ref
        numbers_ref[source_ref.shape[0]] = mask_ref[part.mask_count]
    part.bind(mask_ref[part.mask_count])
    pack_places(part, mask_ref, counts_ref, source_ref, list_ref, start_ref, last_ref, all_ref, other_ref)
    run_pairs(
        part, (0, len(part.lists)), volume_pair, 1, numbers_ref, all_ref,
        own_reader((wide_ref, WIDE)), row_reader(list_ref), kept_ref, before_ref, acc_ref, 2 * GROUP,
    )
    if stage == 3:
        out_ref = refs[-3]
        for index, leaf, sums, valid in leaf_totals(grid, acc_ref, numbers_ref):
            out_ref[leaf] = jnp.where(valid, 1.0 / (1.0 + 4.0 * sums[0]), 1.0)


def density_kernel(grid, part, stage, span, *refs):
    numbers_ref, list_ref, start_ref, last_ref, kept_ref, wide_ref, source_ref = refs[:7]
    before_ref = refs[7] if stage or span[0] else None
    acc_ref = refs[11 if stage == 3 else 8 if before_ref is not None else 7]
    side_ref = refs[-1]
    part.bind(numbers_ref[numbers_ref.shape[0] - 1])
    pack_side(part, span, source_ref, side_ref, start_ref, ())
    run_pairs(
        part, span, density_pair, 3, numbers_ref, last_ref, own_reader((wide_ref, WIDE)),
        row_reader(list_ref, side_ref, 7), kept_ref, before_ref if stage else None, acc_ref,
    )
    if stage == 3:
        own_ref, volume_ref, energy_ref = refs[8:11]
        out_ref = refs[12]
        for (x, y, z), leaf, sums, valid in leaf_totals(grid, acc_ref, numbers_ref):
            density = (own_ref[leaf, 3:4, :] + 4.0 * sums[0]) / (volume_ref[leaf] + 4.0 * sums[1])
            density = jnp.where(valid, density, 1.0)
            energy = energy_ref[x, y, z : z + 1, :]
            out_ref[leaf, 0:1, :] = density
            out_ref[leaf, 1:2, :] = jnp.where(valid, (2.0 / 3.0) * energy / density, 0.0)
            out_ref[leaf, 2:3, :] = jnp.where(valid, jnp.maximum(20.0 * sums[2], 0.0), 0.0)
            out_ref[leaf, 3:4, :] = jnp.zeros_like(density)


def force_kernel(grid, part, stage, span, *refs):
    numbers_ref, list_ref, start_ref, last_ref, kept_ref, wide_ref, state_ref, source_ref = refs[:8]
    before_ref = refs[8] if stage or span[0] else None
    acc_ref = refs[9 if before_ref is not None else 8]
    side_ref = refs[-1]
    part.bind(numbers_ref[numbers_ref.shape[0] - 1])
    pack_side(part, span, source_ref, side_ref, start_ref, (1.0,))
    run_pairs(
        part, span, force_pair, 4, numbers_ref, last_ref,
        own_reader((wide_ref, WIDE), (state_ref, (8, 9, 10))), row_reader(list_ref, side_ref),
        kept_ref, before_ref if stage else None, acc_ref,
    )
    if stage == 3:
        push_ref, heat_ref = refs[10:12]
        for (x, y, z), leaf, sums, valid in leaf_totals(grid, acc_ref, numbers_ref):
            for c in range(3):
                push_ref[x, y, c, z : z + 1, :] = jnp.where(valid, 20.0 * sums[c], 0.0)
            heat_ref[x, y, z : z + 1, :] = jnp.where(valid, -20.0 * sums[3], 0.0)


def call(name, body, inputs, outs, scratch=(), cycles=0, aliases=()):
    def spec(x):
        scalar = x.dtype == jnp.int32 and len(x.shape) == 1
        return pl.BlockSpec(memory_space=pltpu.SMEM if scalar else pltpu.VMEM)

    return pl.pallas_call(
        body,
        out_shape=outs,
        in_specs=[spec(x) for x in inputs],
        out_specs=[spec(x) for x in outs],
        scratch_shapes=scratch,
        input_output_aliases=dict(aliases),
        compiler_params=pltpu.CompilerParams(vmem_limit_bytes=ROOM),
        cost_estimate=pl.CostEstimate(flops=cycles * 4096, bytes_accessed=1 << 20, transcendentals=0),
        name=name,
    )(*inputs)


def floats(*shape):
    return jax.ShapeDtypeStruct(shape, jnp.float32)


def integers(*shape):
    return jax.ShapeDtypeStruct(shape, jnp.int32)


def flat(block):
    return block.reshape((-1,) + block.shape[3:])


def shards(offsets, velocity, mass, energy, partner_mask, counts):
    grid = counts.shape
    slots = offsets.shape[4]
    assert slots == 128
    leaves = grid[0] * grid[1] * grid[2]
    parts = [Layers(grid, part) for part in partners(grid)] + [Side(grid, True), Side(grid, False)]
    inputs = [counts, jnp.swapaxes(offsets, 2, 3), jnp.swapaxes(velocity, 2, 3), mass]
    inputs = [pltpu.with_memory_space_constraint(x, pltpu.HBM) for x in inputs]
    own = pl.pallas_call(
        prepare_kernel,
        out_shape=floats(leaves, 8, slots),
        in_specs=[pl.BlockSpec(memory_space=pltpu.HBM)] * 4,
        out_specs=pl.BlockSpec(memory_space=pltpu.VMEM),
        scratch_shapes=[pltpu.VMEM(x.shape, x.dtype) for x in inputs] + [pltpu.SemaphoreType.DMA((4,))],
        compiler_params=pltpu.CompilerParams(vmem_limit_bytes=ROOM),
        name="prepare",
    )(*inputs)
    one_is_high = jnp.ones((1,), jnp.int32)
    if lax.axis_size("gz") > 2 and lax.axis_size("gz") % 2 == 0:
        one_is_high = 1 - lax.axis_index("gz").astype(jnp.int32)[None] % 2
    mask = jnp.concatenate([partner_mask.reshape(-1), one_is_high])
    wide = call(
        "widen", functools.partial(widen_kernel, WIDE), [own],
        [floats(leaves, len(WIDE), slots, slots)], cycles=2000,
    )[0]

    cut = 3 * leaves // 8

    def side_space(p, height):
        lists = parts[p].lists
        return pltpu.VMEM((len(lists), list_tiles(lists), height, slots), jnp.float32)

    def spread(n_sums):
        return floats(leaves, n_sums, slots, slots)

    def list_outs(p):
        lists = parts[p].lists
        count, tiles = len(lists), list_tiles(lists)
        return [
            floats(count, tiles, 8, slots), integers(count * (longest(lists) + 1)), integers(count),
            floats(count, tiles, slots, slots),
        ]

    numbers, packs = [], []

    def volume_part(p, source, before=()):
        inputs = numbers[:1] + [mask, source, wide, *before]
        outs = [spread(1), integers(source.shape[0] + (p == 0))] + list_outs(p)
        acc, number, *packed = call(
            f"volume_{p}", functools.partial(volume_kernel, grid, parts[p], p), inputs,
            outs + ([floats(leaves, 1, slots)] if p == 3 else []),
            [
                pltpu.SMEM((len(parts[p].lists),), jnp.int32),
                pltpu.SMEM((len(parts[p].lists) * (longest(parts[p].lists) + 1),), jnp.int32),
            ],
            cycles=3000,
            aliases=[(len(inputs) - 1, 0)] if before else (),
        )
        numbers.append(number)
        packs.append(packed[:4])
        return [packed[4] if p == 3 else acc]

    def density_part(p, source, before=(), more=(), span=None):
        span = span or (0, len(parts[p].lists))
        return call(
            f"density_{p}", functools.partial(density_kernel, grid, parts[p], p, span),
            [numbers[0], *packs[p], wide, source, *before, *more],
            [spread(3)] + ([floats(leaves, 4, slots)] if p == 3 else []),
            [side_space(p, 1)], cycles=4000, aliases=[(7, 0)] if before else (),
        )[-1:]

    def force_part(p, source, before=(), span=None):
        span = span or (0, len(parts[p].lists))
        final = [floats(*grid[:2], 3, grid[2], slots), floats(*grid, slots)]
        return call(
            f"force_{p}", functools.partial(force_kernel, grid, parts[p], p, span),
            [numbers[0], *packs[p], wide, wide_state, source, *before],
            [spread(4)] + (final if p == 3 else []),
            [side_space(p, 4)], cycles=5000, aliases=[(8, 0)] if before else (),
        )[-2:]

    early = []

    def keep(run):
        def beside():
            early[:] = run()
            return tuple(early)

        return beside

    layers, one, two, _ = exchange(
        own.reshape(grid + (8, slots)), lambda: (wide,), keep(lambda: volume_part(0, own))
    )
    (volume,) = volume_part(3, two, volume_part(2, one, volume_part(1, layers, early)))

    layers, one, two, _ = exchange(
        volume.reshape(grid + (1, slots)),
        keep(lambda: density_part(0, volume, span=(0, cut))),
        keep(lambda: density_part(0, volume, early, span=(cut, leaves))),
    )
    acc = density_part(2, one, density_part(1, layers, early))
    (state,) = density_part(3, two, acc, [own, volume, energy])

    wide_state = call(
        "widen_state", functools.partial(widen_kernel, (0, 1, 2)), [state],
        [floats(leaves, 3, slots, slots)], cycles=1000,
    )[0]
    layers, one, two, _ = exchange(
        state.reshape(grid + (4, slots)),
        keep(lambda: force_part(0, state, span=(0, cut))),
        keep(lambda: force_part(0, state, early, span=(cut, leaves))),
    )
    push, heat = force_part(3, two, force_part(2, one, force_part(1, layers, early)))
    return jnp.swapaxes(push, 2, 3), heat


def solution(mesh):
    placed = (
        P("gx", "gy", "gz", None, None),
        P("gx", "gy", "gz", None, None),
        P("gx", "gy", "gz", None),
        P("gx", "gy", "gz", None),
        P("gx", "gy", "gz", None),
        P("gx", "gy", "gz"),
    )
    return jax.shard_map(
        shards,
        mesh=mesh,
        in_specs=placed,
        out_specs=(P("gx", "gy", "gz", None, None), P("gx", "gy", "gz", None)),
        check_vma=False,
    )
```

```python
import functools
import itertools

import jax
import jax.numpy as jnp
from jax import lax
from jax.experimental import pallas as pl
from jax.experimental.pallas import tpu as pltpu
from jax.sharding import PartitionSpec as P

AXES = (("gx", 0), ("gy", 1), ("gz", 2))
FAR = 1024.0
TINY = 1e-30
ROOM = 6 << 20
GROUP = 4
WIDE = (0, 1, 2, 4, 5, 6)
OFFSETS = tuple(itertools.product((-1, 0, 1), repeat=3))


def ends_of(block, axis, dim):
    count = lax.axis_size(axis)
    size = block.shape[dim]
    last = lax.slice_in_dim(block, size - 1, None, axis=dim)
    first = lax.slice_in_dim(block, 0, 1, axis=dim)
    if count == 1:
        return first, last, True
    if count == 2:
        ends = block if size == 2 else jnp.concatenate([first, last], axis=dim)
        ends = lax.ppermute(ends, axis, [(0, 1), (1, 0)])
        return lax.slice_in_dim(ends, 0, 1, axis=dim), lax.slice_in_dim(ends, 1, 2, axis=dim), True
    if count % 2:
        forward = [(i, (i + 1) % count) for i in range(count)]
        backward = [(target, source) for source, target in forward]
        return lax.ppermute(first, axis, backward), lax.ppermute(last, axis, forward), True
    even = lax.axis_index(axis) % 2 == 0
    near_pairs = [(i, i + 1 - 2 * (i % 2)) for i in range(count)]
    far_pairs = [(i, (i - 1 + 2 * (i % 2)) % count) for i in range(count)]
    one = lax.ppermute(jnp.where(even, last, first), axis, near_pairs)
    two = lax.ppermute(jnp.where(even, first, last), axis, far_pairs)
    return one, two, even


def low_and_high(block, axis, dim):
    one, two, one_is_high = ends_of(block, axis, dim)
    if one_is_high is True:
        return two, one
    return jnp.where(one_is_high, two, one), jnp.where(one_is_high, one, two)


def after(block, *others):
    return lax.optimization_barrier((block,) + others)[0]


def exchange(block, beside_x, beside_y):
    low, high = low_and_high(block, "gx", 0)
    wide = jnp.concatenate([low, block, high], axis=0)
    first = beside_x()
    low, high = low_and_high(after(wide, *first), "gy", 1)
    layers = jnp.concatenate([low, wide, high], axis=1)
    second = beside_y()
    one, two, one_is_high = ends_of(after(layers, *second), "gz", 2)
    return flat(layers), flat(one), flat(two), one_is_high


def column_constant(values, rows):
    ids = lax.broadcasted_iota(jnp.int32, (rows, 128), 0)
    out = jnp.zeros((rows, 128), jnp.float32)
    for row, value in enumerate(values):
        if value != 0.0:
            out = jnp.where(ids == row, jnp.float32(value), out)
    return out


def apart(own, row):
    return own[0] - row(0), own[1] - row(1), own[2] - row(2)


def volume_pair(own, row, keep):
    dx, dy, dz = apart(own, row)
    square = dx * dx + dy * dy + dz * dz
    radius = square * lax.rsqrt(jnp.maximum(square, TINY))
    inside = jnp.maximum(1.0 - radius, 0.0)
    keep[...] = inside
    second = inside * inside
    return ((second * second) * (1.25 - inside),)


def density_pair(own, row, kept):
    dx, dy, dz = apart(own, row)
    inside = kept[...]
    third = inside * inside * inside
    value = third * (inside * (1.25 - inside))
    relative = (row(4) - own[4]) * dx + (row(5) - own[5]) * dy + (row(6) - own[6]) * dz
    volume = row(7)
    return (
        row(3) * value,
        volume * value,
        (volume * third) * relative,
    )


def force_pair(own, row, kept):
    dx, dy, dz = apart(own, row)
    inside = kept[...]
    scaled = row(3) * (inside * inside * inside)
    relative = (own[4] - row(4)) * dx + (own[5] - row(5)) * dy + (own[6] - row(6)) * dz
    half = (own[10] + row(10)) / (own[8] + row(8))
    heat = own[9] + half
    push = (heat + (row(9) + half)) * scaled
    return (
        push * dx,
        push * dy,
        push * dz,
        (heat * scaled) * relative,
    )


def prepare_kernel(*refs):
    sources, out_ref, holds, sems = refs[:4], refs[4], refs[5:9], refs[9]
    copies = [
        pltpu.make_async_copy(source, hold, sems.at[i])
        for i, (source, hold) in enumerate(zip(sources, holds))
    ]
    for copy in copies:
        copy.start()
    for copy in copies:
        copy.wait()
    counts_ref, offsets_ref, velocity_ref, mass_ref = holds
    nx, ny, nz = mass_ref.shape[:3]
    for leaf, (x, y, z) in enumerate(itertools.product(range(nx), range(ny), range(nz))):
        for c in range(3):
            out_ref[leaf, c : c + 1, :] = offsets_ref[x, y, c, z : z + 1, :]
            out_ref[leaf, 4 + c : 5 + c, :] = velocity_ref[x, y, c, z : z + 1, :]
        out_ref[leaf, 3:4, :] = mass_ref[x, y, z : z + 1, :]
        number = counts_ref[x, y : y + 1, z : z + 1].astype(jnp.float32)
        out_ref[leaf, 7:8, :] = jnp.broadcast_to(number, (1, mass_ref.shape[3]))


def partners(grid):
    nx, ny, nz = grid
    parts = ([], [])
    for x, y, z in itertools.product(range(nx), range(ny), range(nz)):
        for part in parts:
            part.append([])
        for k, (ox, oy, oz) in enumerate(OFFSETS):
            tx, ty, tz = x + ox, y + oy, z + oz
            if 0 <= tz < nz:
                if 0 <= tx < nx and 0 <= ty < ny:
                    parts[0][-1].append((k, (tx * ny + ty) * nz + tz))
                else:
                    parts[1][-1].append((k, ((tx + 1) * (ny + 2) + ty + 1) * nz + tz))
    return parts


class Layers:
    def __init__(self, grid, part):
        self.lists = part
        self.mask_count = 27 * len(part)

    def bind(self, flag):
        self.moves = [column_constant(offset, 8) for offset in OFFSETS]

    def leaf(self, index):
        return index

    def mask_at(self, index, k):
        return index * 27 + k

    def move(self, k):
        return self.moves[k]


class Side:
    def __init__(self, grid, when):
        nx, ny, nz = grid
        self.depth, self.when = nz, when
        self.mask_count = 27 * nx * ny * nz
        columns = [(k, OFFSETS[k][:2]) for k in range(1, 27, 3)]
        self.lists = [
            [(k, (x + ox + 1) * (ny + 2) + y + oy + 1) for k, (ox, oy) in columns]
            for x, y in itertools.product(range(nx), range(ny))
        ]

    def bind(self, flag):
        self.high = flag if self.when else 1 - flag
        heights = lax.broadcasted_iota(jnp.int32, (8, 128), 0)
        along = jnp.where(heights == 2, (2 * self.high - 1).astype(jnp.float32), 0.0)
        self.moves = {k: column_constant(OFFSETS[k][:2], 8) + along for k in range(1, 27, 3)}

    def leaf(self, index):
        return index * self.depth + self.high * (self.depth - 1)

    def mask_at(self, index, k):
        return self.leaf(index) * 27 + (2 * self.high - 1) + k

    def move(self, k):
        return self.moves[k]


def longest(lists):
    return max(len(found) for found in lists)


def list_tiles(lists):
    return longest(lists) + 2


def tile_of(start):
    return lax.shift_right_logical(start, 7)


def from_lane(start, lanes):
    return lanes >= (jnp.broadcast_to(start, lanes.shape) & 127)


def put(list_ref, index, start, block, lanes):
    tile = tile_of(start)
    rolled = pltpu.roll(block, start, axis=1)
    pltpu.store(list_ref.at[index, tile], rolled, mask=from_lane(start, lanes))
    list_ref[index, tile + 1] = rolled


def close(list_ref, index, start, tail, lanes):
    pltpu.store(list_ref.at[index, tile_of(start)], tail, mask=from_lane(start, lanes))


def lane_ids(rows):
    return lax.broadcasted_iota(jnp.int32, (rows, 128), 1)


def pack_places(part, mask_ref, counts_ref, source_ref, list_ref, start_ref, last_ref, all_ref, other_ref):
    stride = longest(part.lists) + 1
    for index, found in enumerate(part.lists):
        kept, other = jnp.int32(0), jnp.int32(0)
        for number, (k, place) in enumerate(found):
            start_ref[index * stride + number] = kept
            other_ref[index * stride + number] = other
            size = counts_ref[place]
            chosen = size * mask_ref[part.mask_at(index, k)]
            kept, other = kept + chosen, other + (size - chosen)
        start_ref[index * stride + len(found)] = kept
        last_ref[index] = tile_of(kept + 127)
        other_ref[index * stride + len(found)] = other
        all_ref[index] = tile_of(kept + other + 127)

    lanes = lane_ids(8)
    only_places = lax.broadcasted_iota(jnp.int32, (8, 128), 0) < 3
    far = column_constant((FAR, FAR, FAR), 8)
    for index, found in enumerate(part.lists):
        for number, (k, place) in enumerate(found):
            put(list_ref, index, start_ref[index * stride + number], source_ref[place] + part.move(k), lanes)
        kept = start_ref[index * stride + len(found)]
        for number, (k, place) in enumerate(found):
            block = jnp.where(only_places, source_ref[place] + part.move(k), 0.0)
            put(list_ref, index, kept + other_ref[index * stride + number], block, lanes)
        close(list_ref, index, kept + other_ref[index * stride + len(found)], far, lanes)


def pack_side(part, span, source_ref, side_ref, start_ref, tail):
    height = source_ref.shape[1]
    lanes = lane_ids(height)
    last = column_constant(tail, height)
    stride = longest(part.lists) + 1
    for index in range(*span):
        found = part.lists[index]
        for number, (_, place) in enumerate(found):
            put(side_ref, index, start_ref[index * stride + number], source_ref[place], lanes)
        close(side_ref, index, start_ref[index * stride + len(found)], last, lanes)


def widen_kernel(rows, block_ref, out_ref):
    for leaf in range(block_ref.shape[0]):
        for index, c in enumerate(rows):
            row = block_ref[leaf, c : c + 1, :]
            out_ref[leaf, index] = jnp.transpose(jnp.broadcast_to(row, (128, 128)))


def read_counts(source_ref, counts_ref):
    for place in range(source_ref.shape[0]):
        counts_ref[place] = source_ref[place, 7:8, :].astype(jnp.int32)[0, 0]


def run_pairs(part, span, pair, n_sums, counts_ref, tiles_ref, own_of, row_of, kept_ref, before_ref, acc_ref, size=GROUP):
    zero = jnp.zeros((8, 128), jnp.float32)

    def leaf_step(index, carry):
        leaf = part.leaf(index)
        count = counts_ref[leaf]
        tiles = tiles_ref[index]

        def group_step(group, carry):
            places = [
                pl.ds(pl.multiple_of(group * (8 * size) + 8 * chunk, 8), 8) for chunk in range(size)
            ]
            owns = [own_of(leaf, at) for at in places]

            def add_tile(tile, sums):
                rows = {}

                def row(c):
                    if c not in rows:
                        rows[c] = jnp.broadcast_to(row_of(index, tile, c), (8, 128))
                    return rows[c]

                terms = [
                    pair(own, row, kept_ref.at[index, tile, at, :]) for own, at in zip(owns, places)
                ]
                return tuple(tuple(a + b for a, b in zip(old, new)) for old, new in zip(sums, terms))

            def two_tiles(step, sums):
                return add_tile(2 * step + 1, add_tile(2 * step, sums))

            start = tuple(
                tuple(zero if before_ref is None else before_ref[leaf, i, at, :] for i in range(n_sums))
                for at in places
            )
            sums = lax.fori_loop(0, lax.shift_right_logical(tiles, 1), two_tiles, start)
            sums = lax.fori_loop(0, tiles & 1, lambda _, sums: add_tile(tiles - 1, sums), sums)
            for at, total in zip(places, sums):
                for i in range(n_sums):
                    acc_ref[leaf, i, at, :] = total[i]
            return carry

        groups = lax.shift_right_logical(count + (8 * size - 1), (8 * size).bit_length() - 1)
        return lax.fori_loop(0, groups, group_step, carry)

    lax.fori_loop(*span, leaf_step, 0)


def lane_sums(blocks):
    return [jnp.sum(jnp.transpose(block), axis=0, keepdims=True) for block in blocks]


def leaf_totals(grid, acc_ref, counts_ref):
    for leaf, index in enumerate(itertools.product(*map(range, grid))):
        sums = lane_sums([acc_ref[leaf, i] for i in range(acc_ref.shape[1])])
        yield index, leaf, sums, lax.broadcasted_iota(jnp.int32, (1, 128), 1) < counts_ref[leaf]


def own_reader(*pieces):
    def own_of(leaf, at):
        return {c: ref[leaf, i, at, :] for ref, channels in pieces for i, c in enumerate(channels)}

    return own_of


def row_reader(list_ref, side_ref=None, base=8):
    def row_of(leaf, at, c):
        if c < base:
            return list_ref[leaf, at, c : c + 1, :]
        return side_ref[leaf, at, c - base : c - base + 1, :]

    return row_of


def volume_kernel(grid, part, stage, *refs):
    refs = list(refs)
    numbers_ref = refs.pop(0) if stage else None
    mask_ref, source_ref, wide_ref = refs[:3]
    before_ref = refs[3] if stage else None
    acc_ref, counts_ref, list_ref, start_ref, last_ref, kept_ref = refs[4 if stage else 3 :][:6]
    all_ref, other_ref = refs[-2:]
    read_counts(source_ref, counts_ref)
    if numbers_ref is None:
        numbers_ref = counts_ref
        numbers_ref[source_ref.shape[0]] = mask_ref[part.mask_count]
    part.bind(mask_ref[part.mask_count])
    pack_places(part, mask_ref, counts_ref, source_ref, list_ref, start_ref, last_ref, all_ref, other_ref)
    run_pairs(
        part, (0, len(part.lists)), volume_pair, 1, numbers_ref, all_ref,
        own_reader((wide_ref, WIDE)), row_reader(list_ref), kept_ref, before_ref, acc_ref, 2 * GROUP,
    )
    if stage == 3:
        out_ref = refs[-3]
        for index, leaf, sums, valid in leaf_totals(grid, acc_ref, numbers_ref):
            out_ref[leaf] = jnp.where(valid, 1.0 / (1.0 + 4.0 * sums[0]), 1.0)


def density_kernel(grid, part, stage, span, *refs):
    numbers_ref, list_ref, start_ref, last_ref, kept_ref, wide_ref, source_ref = refs[:7]
    before_ref = refs[7] if stage or span[0] else None
    acc_ref = refs[11 if stage == 3 else 8 if before_ref is not None else 7]
    side_ref = refs[-1]
    part.bind(numbers_ref[numbers_ref.shape[0] - 1])
    pack_side(part, span, source_ref, side_ref, start_ref, ())
    run_pairs(
        part, span, density_pair, 3, numbers_ref, last_ref, own_reader((wide_ref, WIDE)),
        row_reader(list_ref, side_ref, 7), kept_ref, before_ref if stage else None, acc_ref, 2 * GROUP,
    )
    if stage == 3:
        own_ref, volume_ref, energy_ref = refs[8:11]
        out_ref = refs[12]
        for (x, y, z), leaf, sums, valid in leaf_totals(grid, acc_ref, numbers_ref):
            density = (own_ref[leaf, 3:4, :] + 4.0 * sums[0]) / (volume_ref[leaf] + 4.0 * sums[1])
            density = jnp.where(valid, density, 1.0)
            energy = energy_ref[x, y, z : z + 1, :]
            out_ref[leaf, 0:1, :] = density
            out_ref[leaf, 1:2, :] = jnp.where(valid, (2.0 / 3.0) * energy / density, 0.0)
            out_ref[leaf, 2:3, :] = jnp.where(valid, jnp.maximum(20.0 * sums[2], 0.0), 0.0)
            out_ref[leaf, 3:4, :] = jnp.zeros_like(density)


def force_kernel(grid, part, stage, span, *refs):
    numbers_ref, list_ref, start_ref, last_ref, kept_ref, wide_ref, state_ref, source_ref = refs[:8]
    before_ref = refs[8] if stage or span[0] else None
    acc_ref = refs[9 if before_ref is not None else 8]
    side_ref = refs[-1]
    part.bind(numbers_ref[numbers_ref.shape[0] - 1])
    pack_side(part, span, source_ref, side_ref, start_ref, (1.0,))
    run_pairs(
        part, span, force_pair, 4, numbers_ref, last_ref,
        own_reader((wide_ref, WIDE), (state_ref, (8, 9, 10))), row_reader(list_ref, side_ref),
        kept_ref, before_ref if stage else None, acc_ref,
    )
    if stage == 3:
        push_ref, heat_ref = refs[10:12]
        for (x, y, z), leaf, sums, valid in leaf_totals(grid, acc_ref, numbers_ref):
            for c in range(3):
                push_ref[x, y, c, z : z + 1, :] = jnp.where(valid, 20.0 * sums[c], 0.0)
            heat_ref[x, y, z : z + 1, :] = jnp.where(valid, -20.0 * sums[3], 0.0)


def call(name, body, inputs, outs, scratch=(), cycles=0, aliases=()):
    def spec(x):
        scalar = x.dtype == jnp.int32 and len(x.shape) == 1
        return pl.BlockSpec(memory_space=pltpu.SMEM if scalar else pltpu.VMEM)

    return pl.pallas_call(
        body,
        out_shape=outs,
        in_specs=[spec(x) for x in inputs],
        out_specs=[spec(x) for x in outs],
        scratch_shapes=scratch,
        input_output_aliases=dict(aliases),
        compiler_params=pltpu.CompilerParams(
            vmem_limit_bytes=ROOM
        ),
        cost_estimate=pl.CostEstimate(flops=cycles * 4096, bytes_accessed=1 << 20, transcendentals=0),
        name=name,
    )(*inputs)


def floats(*shape):
    return jax.ShapeDtypeStruct(shape, jnp.float32)


def integers(*shape):
    return jax.ShapeDtypeStruct(shape, jnp.int32)


def flat(block):
    return block.reshape((-1,) + block.shape[3:])


def shards(offsets, velocity, mass, energy, partner_mask, counts):
    grid = counts.shape
    slots = offsets.shape[4]
    assert slots == 128
    leaves = grid[0] * grid[1] * grid[2]
    parts = [Layers(grid, part) for part in partners(grid)] + [Side(grid, True), Side(grid, False)]
    inputs = [counts, jnp.swapaxes(offsets, 2, 3), jnp.swapaxes(velocity, 2, 3), mass]
    inputs = [pltpu.with_memory_space_constraint(x, pltpu.HBM) for x in inputs]
    own = pl.pallas_call(
        prepare_kernel,
        out_shape=floats(leaves, 8, slots),
        in_specs=[pl.BlockSpec(memory_space=pltpu.HBM)] * 4,
        out_specs=pl.BlockSpec(memory_space=pltpu.VMEM),
        scratch_shapes=[pltpu.VMEM(x.shape, x.dtype) for x in inputs] + [pltpu.SemaphoreType.DMA((4,))],
        compiler_params=pltpu.CompilerParams(vmem_limit_bytes=ROOM),
        name="prepare",
    )(*inputs)
    one_is_high = jnp.ones((1,), jnp.int32)
    if lax.axis_size("gz") > 2 and lax.axis_size("gz") % 2 == 0:
        one_is_high = 1 - lax.axis_index("gz").astype(jnp.int32)[None] % 2
    mask = jnp.concatenate([partner_mask.reshape(-1), one_is_high])
    wide = call(
        "widen", functools.partial(widen_kernel, WIDE), [own],
        [floats(leaves, len(WIDE), slots, slots)], cycles=2000,
    )[0]

    cut = 3 * leaves // 8

    def side_space(p, height):
        lists = parts[p].lists
        return pltpu.VMEM((len(lists), list_tiles(lists), height, slots), jnp.float32)

    def spread(n_sums):
        return floats(leaves, n_sums, slots, slots)

    def list_outs(p):
        lists = parts[p].lists
        count, tiles = len(lists), list_tiles(lists)
        return [
            floats(count, tiles, 8, slots), integers(count * (longest(lists) + 1)), integers(count),
            floats(count, tiles, slots, slots),
        ]

    numbers, packs = [], []

    def volume_part(p, source, before=()):
        inputs = numbers[:1] + [mask, source, wide, *before]
        outs = [spread(1), integers(source.shape[0] + (p == 0))] + list_outs(p)
        acc, number, *packed = call(
            f"volume_{p}", functools.partial(volume_kernel, grid, parts[p], p), inputs,
            outs + ([floats(leaves, 1, slots)] if p == 3 else []),
            [
                pltpu.SMEM((len(parts[p].lists),), jnp.int32),
                pltpu.SMEM((len(parts[p].lists) * (longest(parts[p].lists) + 1),), jnp.int32),
            ],
            cycles=3000,
            aliases=[(len(inputs) - 1, 0)] if before else (),
        )
        numbers.append(number)
        packs.append(packed[:4])
        return [packed[4] if p == 3 else acc]

    def density_part(p, source, before=(), more=(), span=None):
        span = span or (0, len(parts[p].lists))
        return call(
            f"density_{p}", functools.partial(density_kernel, grid, parts[p], p, span),
            [numbers[0], *packs[p], wide, source, *before, *more],
            [spread(3)] + ([floats(leaves, 4, slots)] if p == 3 else []),
            [side_space(p, 1)], cycles=4000, aliases=[(7, 0)] if before else (),
        )[-1:]

    def force_part(p, source, before=(), span=None):
        span = span or (0, len(parts[p].lists))
        final = [floats(*grid[:2], 3, grid[2], slots), floats(*grid, slots)]
        return call(
            f"force_{p}", functools.partial(force_kernel, grid, parts[p], p, span),
            [numbers[0], *packs[p], wide, wide_state, source, *before],
            [spread(4)] + (final if p == 3 else []),
            [side_space(p, 4)], cycles=5000, aliases=[(8, 0)] if before else (),
        )[-2:]

    early = []

    def keep(run):
        def beside():
            early[:] = run()
            return tuple(early)

        return beside

    layers, one, two, _ = exchange(
        own.reshape(grid + (8, slots)), lambda: (wide,), keep(lambda: volume_part(0, own))
    )
    (volume,) = volume_part(3, two, volume_part(2, one, volume_part(1, layers, early)))

    layers, one, two, _ = exchange(
        volume.reshape(grid + (1, slots)),
        keep(lambda: density_part(0, volume, span=(0, cut))),
        keep(lambda: density_part(0, volume, early, span=(cut, leaves))),
    )
    acc = density_part(2, one, density_part(1, layers, early))
    (state,) = density_part(3, two, acc, [own, volume, energy])

    wide_state = call(
        "widen_state", functools.partial(widen_kernel, (0, 1, 2)), [state],
        [floats(leaves, 3, slots, slots)], cycles=1000,
    )[0]
    layers, one, two, _ = exchange(
        state.reshape(grid + (4, slots)),
        keep(lambda: force_part(0, state, span=(0, cut))),
        keep(lambda: force_part(0, state, early, span=(cut, leaves))),
    )
    push, heat = force_part(3, two, force_part(2, one, force_part(1, layers, early)))
    return jnp.swapaxes(push, 2, 3), heat


def solution(mesh):
    placed = (
        P("gx", "gy", "gz", None, None),
        P("gx", "gy", "gz", None, None),
        P("gx", "gy", "gz", None),
        P("gx", "gy", "gz", None),
        P("gx", "gy", "gz", None),
        P("gx", "gy", "gz"),
    )
    return jax.shard_map(
        shards,
        mesh=mesh,
        in_specs=placed,
        out_specs=(P("gx", "gy", "gz", None, None), P("gx", "gy", "gz", None)),
        check_vma=False,
    )
```
